512 devices in a mesh: tile: 8 (over x, core), member: 4 (over y), region: 16 (over z).
Axes of the slice: x: 4, y: 4, z: 16, core: 2. Of those that a mesh axis runs over, the one named last changes fastest.
Arguments:
- background: float32 [80, 128, 8192], P('member', 'region', 'tile'), may hold values from -25 to 25
- obs_cell: int32 [16, 1024], P('region', 'tile'), may hold values from 0 to 8191
- obs_weight: float32 [4, 16, 1024], P(None, 'region', 'tile'), may hold values from 0.05 to 1
- obs_value: float32 [16, 1024], P('region', 'tile'), may hold values from -6 to 6
- obs_error: float32 [16, 1024], P('region', 'tile'), may hold values from 16 to 170
- obs_count: int32 [16, 8], P('region', 'tile'), may hold values from 1 to 128, as said below
- obs_batch: int32 [16, 1024], P('region', 'tile'), may hold values 0 or 1
Outputs:
- analysis: float32 [80, 128, 8192], P(None, 'region', ('tile', 'member'))
The draws below stay inside these ranges and needn't reach their ends.
Inputs may be any that keep to these rules, and one draw needn't show every extreme that they name: `obs_count`: the live observations of one region and tile fill its leading slots; some region and tile has all 128 slots live in every draw.
All inputs are finite; a program needn't handle non-finite values. No bound on the sum of `obs_batch` on one device may be relied on, other than what follows from the above.
Results may differ from the reference program's by a relative error of at most 0.00011.
Values sent between devices are 32-bit elements; how exact they have to be, the bound alone decides.
A program may use at most 64 MiB of HBM per device.

```python
import math
import jax
import jax.numpy as jnp
from jax import lax

MEMBERS = 80
ROW_DEV = 8
CELL_DEV = 1024
OBS_DEV = 128
REGIONS = 16
TILES = 8
ROWS = 128
CELLS = 8192
SLOTS = 1024


def draw_background(key, part):
    member_key = jax.random.fold_in(key, 11)
    pattern_key = jax.random.fold_in(key, 12)
    region_key = jax.random.fold_in(key, 13)
    noise_key = jax.random.fold_in(key, 14)
    factor = jax.random.uniform(member_key, (MEMBERS, 1, 1), jnp.float32, -1.7, 1.7)
    pattern = 0.6 * jnp.clip(jax.random.normal(pattern_key, (1, ROWS, CELLS), jnp.float32), -3.0, 3.0)
    logs = jax.random.uniform(region_key, (REGIONS,), jnp.float32, math.log(0.3), math.log(3.3))
    region_scale = jnp.repeat(jnp.exp(logs), ROW_DEV)[None, :, None]
    noise = jnp.clip(jax.random.normal(noise_key, (MEMBERS, ROWS, CELLS), jnp.float32), -4.0, 4.0)
    return (region_scale * (factor * pattern + noise)).astype(jnp.float32)


def draw_obs_count(key, part):
    halving = jax.random.randint(key, (REGIONS * TILES,), 0, 4)
    counts = jnp.right_shift(jnp.full((REGIONS * TILES,), OBS_DEV, jnp.int32), halving.astype(jnp.int32))
    chosen = jax.random.randint(jax.random.fold_in(key, 7), (), 0, REGIONS * TILES)
    counts = jnp.where(jnp.arange(REGIONS * TILES) == chosen, OBS_DEV, counts)
    return jnp.maximum(counts, 1).reshape(REGIONS, TILES).astype(jnp.int32)


def touch_ends(drawn, stream_key, low, largest):
    shape = drawn.shape
    spot = [jax.random.randint(jax.random.fold_in(stream_key, axis), (), 0, shape[axis]) for axis in range(len(shape))]
    drawn = drawn.at[tuple(spot)].set(low)
    longest = shape.index(max(shape))
    spot[longest] = (spot[longest] + 1) % shape[longest]
    return drawn.at[tuple(spot)].set(largest)


def level_of(key, dims, split, least, top_value):
    level, own = 1.0, jax.random.fold_in(key, 6)
    for axis_at, shards_of in split:
        steps = jnp.exp(jax.random.uniform(jax.random.fold_in(own, axis_at), (shards_of,), jnp.float32, least / len(split), top_value / len(split)))
        level = level * jnp.repeat(steps, dims[axis_at] // shards_of).reshape([-1 if axis == axis_at else 1 for axis in range(len(dims))])
    return level


def normal_values(own_key, extent, scale, limit, split=(), kind=jnp.bfloat16):
    gain = level_of(own_key, extent, split, -0.22, 0.18) if split else 1.0
    drawn = jax.random.normal(own_key, extent, jnp.float32) * scale * gain
    return jnp.minimum(jnp.maximum(drawn, -limit), limit).astype(kind)


def setup_inputs(seed: int = 0) -> dict:
    streams_of = jax.random.split(jax.random.key(seed), 8)
    background = draw_background(jax.random.fold_in(streams_of[7], 71), 0)
    obs_cell = touch_ends(jax.random.randint(streams_of[1], (REGIONS, SLOTS), 0, ROW_DEV * CELL_DEV), jax.random.fold_in(streams_of[1], 1), 0, (ROW_DEV * CELL_DEV) - 1).astype(jnp.int32)
    obs_weight = jnp.clip(0.05 + 0.95 * jax.random.uniform(streams_of[2], (4, REGIONS, SLOTS), jnp.float32) ** level_of(streams_of[2], (4, REGIONS, SLOTS), ((1, 16), (2, 8)), -0.2, 0.2), 0.05, 1.0)
    obs_value = normal_values(streams_of[3], (REGIONS, SLOTS), 1.0, 6.0, ((0, 16), (1, 8)), jnp.float32)
    obs_error = jnp.clip(jnp.exp(math.log(170.0) - 2.3632097 * jax.random.uniform(streams_of[4], (REGIONS, SLOTS), jnp.float32) ** level_of(streams_of[4], (REGIONS, SLOTS), ((0, 16), (1, 8)), -0.2, 0.2)), 16.0, 170.0)
    obs_count = draw_obs_count(jax.random.fold_in(streams_of[7], 71), 0)
    obs_batch = touch_ends((jax.random.randint(streams_of[6], (REGIONS, SLOTS), 0, 2) < 1).astype(jnp.int32), jax.random.fold_in(streams_of[6], 1), 0, 1)
    return {"background": background, "obs_cell": obs_cell, "obs_weight": obs_weight, "obs_value": obs_value, "obs_error": obs_error, "obs_count": obs_count, "obs_batch": obs_batch}


EXACT = lax.Precision.HIGHEST

def locality(regions):
    positions = jnp.arange(regions, dtype=jnp.float32)
    distance = (positions[:, None] - positions[None, :]) * (4.0 / regions)
    return jnp.exp(-0.5 * distance * distance)

def transform(covariance, innovation, members):
    identity = jnp.eye(members, dtype=jnp.float32)
    system = (members - 1.0) * identity + covariance
    factor = jnp.linalg.cholesky(system)
    inverse = lax.linalg.triangular_solve(factor, jnp.broadcast_to(identity, factor.shape), left_side=True, lower=True)
    partial_solve = jnp.einsum('kij,kj->ki', inverse, innovation, precision=EXACT)
    weights = jnp.einsum('kji,kj->ki', inverse, partial_solve, precision=EXACT)
    square_root = math.sqrt(members - 1.0) * jnp.swapaxes(inverse, 1, 2)
    center = identity - 1.0 / members
    combined = weights[:, :, None] + square_root
    return 1.0 / members + jnp.einsum('ij,kjl->kil', center, combined, precision=EXACT)

def statistics(priors, values, scale):
    average = lax.optimization_barrier(jnp.mean(priors, axis=0))
    spread = priors - average
    weighted = spread * scale
    covariance = jnp.einsum('mrs,nrs->rmn', weighted, spread, precision=EXACT)
    innovation = jnp.einsum('mrs,rs->rm', weighted, values - average, precision=EXACT)
    return (covariance, innovation)

def localized(near, covariance, innovation):
    return (jnp.einsum('rs,smn->rmn', near, covariance, precision=EXACT), jnp.dot(near, innovation, precision=EXACT))

def reference(background, obs_cell, obs_weight, obs_value, obs_error, obs_count, obs_batch):
    members = MEMBERS
    width = CELLS + 4
    padded = jnp.pad(background, ((0, 0), (0, 0), (2, 2)))
    flat = padded.reshape(members, -1)
    slot_index = jnp.arange(SLOTS, dtype=jnp.int32)
    tile_of = (slot_index // OBS_DEV).astype(jnp.int32)
    row_global = jnp.arange(REGIONS, dtype=jnp.int32)[:, None] * ROW_DEV + obs_cell // CELL_DEV
    col_global = tile_of[None, :] * CELL_DEV + obs_cell % CELL_DEV + 1
    start = (row_global * width + col_global).astype(jnp.int32)
    priors = jnp.zeros((members, REGIONS, SLOTS), jnp.float32)
    for offset in range(4):
        taken = jnp.take(flat, (start + offset).reshape(-1), axis=1).reshape(members, REGIONS, SLOTS)
        priors = priors + obs_weight[offset][None] * taken
    filled = (slot_index % OBS_DEV)[None, :] < jnp.repeat(obs_count, OBS_DEV, axis=1)
    scale_one = jnp.where(filled & (obs_batch == 0), 1.0 / obs_error, 0.0)
    scale_two = jnp.where(filled & (obs_batch == 1), 1.0 / obs_error, 0.0)
    near = locality(REGIONS)
    cov_one, inn_one = statistics(priors, obs_value, scale_one)
    first = transform(*localized(near, cov_one, inn_one), members)
    updated = jnp.einsum('nrs,rnm->mrs', priors, first, precision=EXACT)
    cov_two, inn_two = statistics(updated, obs_value, scale_two)
    second = transform(*localized(near, cov_two, inn_two), members)
    blocks = background.reshape(members, REGIONS, ROW_DEV * CELLS)
    middle = jnp.einsum('nrc,rnm->mrc', blocks, first, precision=EXACT)
    result = jnp.einsum('nrc,rnm->mrc', middle, second, precision=EXACT)
    return result.reshape(members, ROWS, CELLS)
```

```python
import functools
import math

import jax
import jax.numpy as jnp
from jax import lax
from jax.experimental import pallas as pl
from jax.experimental.pallas import tpu as pltpu
from jax.sharding import PartitionSpec as P

EXACT = lax.Precision.HIGHEST
MESH = pl.DeviceIdType.MESH
F32 = jnp.float32
BF16 = jnp.bfloat16
MEMBERS = 80
TILES, SPLIT, REGIONS = 8, 4, 16
PART = MEMBERS // SPLIT
NT = (((1,), (1,)), ((), ()))


def rem(a, n):
    return lax.rem(a, n)


def iota(shape, dim):
    return lax.broadcasted_iota(jnp.int32, shape, dim)


def halves(a):
    high = a.astype(BF16)
    low = (a - high.astype(F32)).astype(BF16)
    return high, low


def left_operand(a):
    lane = iota(a.shape, 1)
    high = a.astype(BF16).astype(F32)
    low = a - high
    turned = pltpu.roll(high, MEMBERS, 1)
    one = jnp.where(lane < MEMBERS, high, turned)
    two = jnp.where(lane < 32, turned, pltpu.roll(low, 32, 1))
    return jnp.concatenate([one, two], axis=1).astype(BF16)


def eliminated(groups):
    lane, sub = iota((8, 128), 1), iota((8, 128), 0)
    groups = list(groups)
    for k in range(MEMBERS):
        first, s = divmod(k, 8)
        row = jnp.broadcast_to(groups[first][s : s + 1, :], (8, 128))
        pivot = jnp.broadcast_to(row[:, k : k + 1], (8, 128))
        here = lane == k
        scaled = jnp.where(here, 1.0, row) * (1.0 / pivot)
        for g in range(first, 10):
            column = jnp.broadcast_to(groups[g][:, k : k + 1], (8, 128))
            changed = jnp.where(here, 0.0, groups[g]) - column * scaled
            groups[g] = jnp.where(sub > s, changed, groups[g]) if g == first else changed
    return jnp.concatenate(groups, axis=0)


def transform_rows(system_ref):
    lane, row = iota((MEMBERS, 128), 1), iota((MEMBERS, 128), 0)
    system = system_ref[0:MEMBERS, :] + jnp.where(lane == row, MEMBERS - 1.0, 0.0)
    done = eliminated([system[8 * g : 8 * g + 8, :] for g in range(10)])
    diagonal = jnp.sum(jnp.where(lane == row, done, 0.0), axis=1, keepdims=True)
    root = lax.rsqrt(diagonal)
    inverse = jnp.where(lane < row, done, jnp.where(lane == row, 1.0, 0.0)) * root
    partial = jnp.sum(jnp.where(lane == MEMBERS, done, 0.0), axis=1, keepdims=True) * root
    weights = jnp.sum(inverse * partial, axis=0, keepdims=True)
    live = lane < MEMBERS
    weights = weights - jnp.sum(weights, axis=1, keepdims=True) / MEMBERS
    centered = math.sqrt(MEMBERS - 1.0) * (inverse - jnp.sum(inverse, axis=1, keepdims=True) / MEMBERS)
    rows = jnp.where(live, centered + weights + 1.0 / MEMBERS, 0.0)
    return rows


def kernel(
    bg, cell, wgt, val, err, cnt, bat, out,
    bgv, x, xcat, outv, halo, from_left, from_right, mine, priors, full, spread, parts, shares,
    own, zone, bslots, bfull, mixed, cslots, system, own2, zone2, mixed2, cslots2, system2,
    load_sem, bulk_s, bulk_r, halo_s, left_r, right_r, prior_s, prior_r, share_s, share_r,
    zone_s, zone_r, b_s, b_r, c_s, c_r, zone2_s, zone2_r, c2_s, c2_r,
):
    t, y, z = lax.axis_index("tile"), lax.axis_index("member"), lax.axis_index("region")
    core, q = rem(t, 2), 4 * y + lax.div(t, 2)

    def at(dt, dy, dz):
        return {
            "tile": rem(t + dt, TILES),
            "member": rem(y + dy, SPLIT),
            "region": rem(z + dz, REGIONS),
        }

    def push(src, dst, s, r, where):
        copy = pltpu.make_async_remote_copy(
            src_ref=src, dst_ref=dst, send_sem=s, recv_sem=r, device_id=where, device_id_type=MESH
        )
        return copy

    plane = [(dt, dy) for dy in range(SPLIT) for dt in range(TILES) if (dt, dy) != (0, 0)]
    peers = [(dt, dy, 0) for dt, dy in plane] + [(0, 0, dz) for dz in range(1, REGIONS)]

    load = pltpu.make_async_copy(bg, bgv, load_sem.at[0])
    load.start()
    barrier = pltpu.get_barrier_semaphore()
    for dt, dy, dz in peers:
        pl.semaphore_signal(barrier, inc=1, device_id=at(dt, dy, dz), device_id_type=MESH)

    place = cell[...]
    at_row, at_col = lax.shift_right_logical(place, 10), place & 1023
    w = [wgt[k] for k in range(4)]
    step = iota((1024, 128), 0) - (at_col - 1)
    taps = jnp.where(step == 0, w[0], jnp.where(step == 1, w[1], jnp.where(step == 2, w[2], jnp.where(step == 3, w[3], 0.0))))
    filled = iota((1, 128), 1) < cnt[...]
    inverse_error = 1.0 / err[...]
    scales = [jnp.where(filled & (bat[...] == b), inverse_error, 0.0) for b in range(2)]
    load.wait()

    packed = jnp.zeros((8, 128), F32)
    lane8 = iota((8, 128), 1)
    for a in range(3):
        count = min(8, PART - 8 * a)
        for r in range(8):
            ends = [bgv[8 * a : 8 * a + count, r, c : c + 128] for c in (896, 0)]
            if count < 8:
                ends = [jnp.concatenate([e, jnp.zeros((8 - count, 128), F32)], axis=0) for e in ends]
            for j, (end, lane) in enumerate(((ends[0], 127), (ends[1], 0), (ends[1], 1))):
                target = 32 * a + 8 * j + r
                packed = jnp.where(lane8 == target, pltpu.roll(end, (target - lane) % 128, 1), packed)
    halo[...] = packed

    rows = bgv[...].reshape(PART * 8, 1024)
    taken = jnp.dot(rows, taps, precision=EXACT, preferred_element_type=F32).reshape(PART, 8, 128)
    chosen = iota((8, 128), 0) == at_row
    mine[...] = jnp.zeros_like(mine)
    mine[0:PART, :] = jnp.sum(jnp.where(chosen[None], taken, 0.0), axis=1)

    near = []
    for d in range(REGIONS):
        other = rem(z - d + REGIONS, REGIONS)
        distance = jnp.full((8, 128), z - other, jnp.int32).astype(F32) * (4.0 / REGIONS)
        near.append(jnp.exp(-0.5 * distance * distance))

    pl.semaphore_wait(barrier, len(peers))

    sent = []

    def go(copy):
        copy.start()
        sent.append(copy)

    for i in range(1, SPLIT):
        go(push(mine, priors.at[y], prior_s.at[i - 1], prior_r.at[y], at(0, i, 0)))
    for i in range(SPLIT):
        go(push(halo, from_left.at[y], halo_s.at[i], left_r.at[y], at(1, i, 0)))
        go(push(halo, from_right.at[y], halo_s.at[4 + i], right_r.at[y], at(TILES - 1, i, 0)))
    for i in range(1, SPLIT):
        to = rem(y + i, SPLIT)
        columns = pl.ds(pl.multiple_of(to * 256, 256), 256)
        go(push(bgv.at[:, :, columns], x.at[pl.ds(y * PART, PART)], bulk_s.at[i - 1], bulk_r.at[y], at(0, i, 0)))
    keep = pltpu.make_async_copy(
        bgv.at[:, :, pl.ds(pl.multiple_of(y * 256, 256), 256)], x.at[pl.ds(y * PART, PART)], load_sem.at[1]
    )
    keep.start()
    priors[y] = mine[...]

    v = [
        jnp.where((t > 0) & (at_col == 0), w[0], 0.0),
        jnp.where(t < TILES - 1, jnp.where(at_col == 1023, w[2], jnp.where(at_col == 1022, w[3], 0.0)), 0.0),
        jnp.where((t < TILES - 1) & (at_col == 1023), w[3], 0.0),
    ]
    block = jnp.concatenate([jnp.where(chosen, value, 0.0) for value in v] + [jnp.zeros((8, 128), F32)], axis=0)
    nothing = jnp.zeros((32, 128), F32)
    spots = jnp.concatenate(
        [jnp.concatenate([block if b == a else nothing for b in range(4)], axis=0) for a in range(3)], axis=1
    )
    for i in range(SPLIT):
        push(halo, from_left.at[i], halo_s.at[0], left_r.at[i], at(0, 0, 0)).wait_recv()
        push(halo, from_right.at[i], halo_s.at[0], right_r.at[i], at(0, 0, 0)).wait_recv()
    from_j0 = (lane8 & 31) < 8
    sides = jnp.concatenate([jnp.where(from_j0, from_left[i], from_right[i]) for i in range(SPLIT)], axis=0)
    extra = jnp.dot(sides, spots, precision=EXACT, preferred_element_type=F32)
    for i in range(1, SPLIT):
        it = rem(y + i, SPLIT)
        push(mine, priors.at[it], prior_s.at[0], prior_r.at[it], at(0, 0, 0)).wait_recv()
    for i in range(SPLIT):
        for a in range(3):
            full[PART * i + 8 * a : PART * i + 8 * a + 8, :] = (
                priors[i, 8 * a : 8 * a + 8, :] + extra[8 * i : 8 * i + 8, 128 * a : 128 * a + 128]
            )
    ensemble = full[0:MEMBERS, :]
    average = jnp.sum(ensemble, axis=0, keepdims=True) / MEMBERS
    spread[MEMBERS : 128, :] = jnp.where(iota((48, 128), 0) == 0, val[...] - average, 0.0)
    spread[0:MEMBERS, :] = ensemble - average
    picks = []
    for c in range(8):
        start = y * PART + 5 * (c // 2)
        picks.append(spread[pl.ds(start, 8), :] * scales[c % 2])
    products = lax.dot_general(
        jnp.concatenate(picks, axis=0), spread[...], NT, precision=EXACT, preferred_element_type=F32
    )
    for c in range(8):
        parts[c] = products[8 * c : 8 * c + 8, :]
    for d in range(1, TILES):
        to = rem(t + d, TILES)
        go(push(parts.at[to], shares.at[d - 1], share_s.at[d - 1], share_r.at[d - 1], at(d, 0, 0)))
    total = parts[t]
    for d in range(1, TILES):
        push(parts.at[0], shares.at[d - 1], share_s.at[0], share_r.at[d - 1], at(0, 0, 0)).wait_recv()
    for d in range(1, TILES):
        total = total + shares[d - 1]
    own[...] = total

    def to_plane(src, slots, s, r):
        return [push(src, slots.at[q], s.at[i], r.at[q], at(dt, dy, 0)) for i, (dt, dy) in enumerate(plane)]

    def to_zone(src, slots, s, r):
        return [push(src, slots.at[d - 1], s.at[d - 1], r.at[d - 1], at(0, 0, d)) for d in range(1, REGIONS)]

    def mix(src, slots, s, r):
        for d in range(1, REGIONS):
            push(src, slots.at[d - 1], s.at[0], r.at[d - 1], at(0, 0, 0)).wait_recv()
        result = near[0] * src[...]
        for d in range(1, REGIONS):
            result = result + near[d] * slots[d - 1]
        return result

    def gathered(src, slots, s, r, owner, whole):
        for p in range(16):
            @pl.when((core != owner) | (q != p))
            def _():
                push(src, slots.at[p], s.at[0], r.at[p], at(0, 0, 0)).wait_recv()
        for p in range(16):
            whole[5 * p : 5 * p + 8, :] = slots[p]

    b_copies = to_plane(own, bslots, b_s, b_r)
    z_copies = to_zone(own, zone, zone_s, zone_r)
    c_copies = to_plane(mixed, cslots, c_s, c_r)
    z2_copies = to_zone(own2, zone2, zone2_s, zone2_r)
    c2_copies = to_plane(mixed2, cslots2, c2_s, c2_r)

    @pl.when(core == 0)
    def _():
        for copy in z_copies:
            copy.start()
        mixed[...] = mix(own, zone, zone_s, zone_r)
        for copy in c_copies:
            copy.start()
        cslots[q] = mixed[...]

    @pl.when(core == 1)
    def _():
        for copy in b_copies:
            copy.start()
        bslots[q] = own[...]

    gathered(own, bslots, b_s, b_r, 1, bfull)
    bfull[MEMBERS : 128, :] = jnp.zeros((48, 128), F32)
    gathered(mixed, cslots, c_s, c_r, 0, system)
    first = transform_rows(system)

    lane, row = iota((MEMBERS, 128), 1), iota((MEMBERS, 128), 0)
    mean_row = jnp.sum(first, axis=0, keepdims=True) / MEMBERS
    system[0:MEMBERS, :] = first - mean_row
    left = jnp.dot(system[pl.ds(5 * q, 8), :], bfull[...], precision=EXACT, preferred_element_type=F32)
    right = jnp.concatenate(
        [system[0:MEMBERS, :], jnp.where(iota((48, 128), 0) == 0, mean_row, 0.0)], axis=0
    )
    stats = lax.dot_general(
        jnp.where(lane8 < MEMBERS, left, 0.0), right, NT, precision=EXACT, preferred_element_type=F32
    )
    own2[...] = jnp.where(lane8 == MEMBERS, left - stats, stats)

    @pl.when(core == 0)
    def _():
        for copy in z2_copies:
            copy.start()

    keep.wait()
    for i in range(1, SPLIT):
        it = rem(y + i, SPLIT)
        push(
            bgv.at[:, :, 0:256], x.at[pl.ds(it * PART, PART)], bulk_s.at[0], bulk_r.at[it], at(0, 0, 0)
        ).wait_recv()
    first_left = left_operand(first)
    blank = jnp.zeros((16, 256), BF16)
    for r in range(8):
        high, low = halves(x[:, r, :])
        middle = jnp.dot(first_left, jnp.concatenate([high, low, high, blank], axis=0), preferred_element_type=F32)
        high, low = halves(middle)
        xcat[r, 0:80, :] = high
        xcat[r, 80:160, :] = low
        xcat[r, 160:240, :] = high
        xcat[r, 240:256, :] = blank

    @pl.when(core == 0)
    def _():
        mixed2[...] = mix(own2, zone2, zone2_s, zone2_r)
        for copy in c2_copies:
            copy.start()
        cslots2[q] = mixed2[...]

    gathered(mixed2, cslots2, c2_s, c2_r, 0, system2)
    second_left = left_operand(transform_rows(system2))
    for r in range(8):
        outv[:, r, :] = jnp.dot(second_left, xcat[r], preferred_element_type=F32)
    store = pltpu.make_async_copy(outv, out, load_sem.at[2])
    store.start()
    for copy in sent:
        copy.wait_send()

    @pl.when(core == 0)
    def _():
        for copy in z_copies + c_copies + z2_copies + c2_copies:
            copy.wait_send()

    @pl.when(core == 1)
    def _():
        for copy in b_copies:
            copy.wait_send()

    store.wait()


def shards(background, obs_cell, obs_weight, obs_value, obs_error, obs_count, obs_batch):
    vmem = pl.BlockSpec(memory_space=pltpu.VMEM)
    hbm = pl.BlockSpec(memory_space=pl.ANY)
    tile = (8, 128)
    dma = pltpu.SemaphoreType.DMA
    return pl.pallas_call(
        kernel,
        out_shape=jax.ShapeDtypeStruct((MEMBERS, 8, 256), F32),
        in_specs=[hbm] + [vmem] * 6,
        out_specs=hbm,
        scratch_shapes=[
            pltpu.VMEM((PART, 8, 1024), F32),
            pltpu.VMEM((MEMBERS, 8, 256), F32),
            pltpu.VMEM((8, 256, 256), BF16),
            pltpu.VMEM((MEMBERS, 8, 256), F32),
            pltpu.VMEM(tile, F32),
            pltpu.VMEM((SPLIT, *tile), F32),
            pltpu.VMEM((SPLIT, *tile), F32),
            pltpu.VMEM((24, 128), F32),
            pltpu.VMEM((SPLIT, 24, 128), F32),
            pltpu.VMEM((88, 128), F32),
            pltpu.VMEM((128, 128), F32),
            pltpu.VMEM((TILES, *tile), F32),
            pltpu.VMEM((TILES - 1, *tile), F32),
            pltpu.VMEM(tile, F32),
            pltpu.VMEM((REGIONS - 1, *tile), F32),
            pltpu.VMEM((16, *tile), F32),
            pltpu.VMEM((128, 128), F32),
            pltpu.VMEM(tile, F32),
            pltpu.VMEM((16, *tile), F32),
            pltpu.VMEM((88, 128), F32),
            pltpu.VMEM(tile, F32),
            pltpu.VMEM((REGIONS - 1, *tile), F32),
            pltpu.VMEM(tile, F32),
            pltpu.VMEM((16, *tile), F32),
            pltpu.VMEM((88, 128), F32),
            dma((3,)), dma((3,)), dma((4,)), dma((8,)), dma((4,)), dma((4,)), dma((3,)), dma((4,)),
            dma((7,)), dma((7,)), dma((15,)), dma((15,)), dma((31,)), dma((16,)), dma((31,)), dma((16,)),
            dma((15,)), dma((15,)), dma((31,)), dma((16,)),
        ],
        compiler_params=pltpu.CompilerParams(
            collective_id=0, has_side_effects=True, vmem_limit_bytes=48 * 1024 * 1024
        ),
    )(background, obs_cell, obs_weight, obs_value, obs_error, obs_count, obs_batch)


def solution(mesh):
    return jax.shard_map(
        shards,
        mesh=mesh,
        in_specs=(
            P("member", "region", "tile"),
            P("region", "tile"),
            P(None, "region", "tile"),
            P("region", "tile"),
            P("region", "tile"),
            P("region", "tile"),
            P("region", "tile"),
        ),
        out_specs=P(None, "region", ("tile", "member")),
        check_vma=False,
    )
```

```python
import functools
import math

import jax
import jax.numpy as jnp
from jax import lax
from jax.experimental import pallas as pl
from jax.experimental.pallas import tpu as pltpu
from jax.sharding import PartitionSpec as P

EXACT = lax.Precision.HIGHEST
MESH = pl.DeviceIdType.MESH
F32 = jnp.float32
BF16 = jnp.bfloat16
MEMBERS = 80
TILES, SPLIT, REGIONS = 8, 4, 16
PART = MEMBERS // SPLIT
NT = (((1,), (1,)), ((), ()))


def rem(a, n):
    return lax.rem(a, n)


def iota(shape, dim):
    return lax.broadcasted_iota(jnp.int32, shape, dim)


def halves(a):
    high = a.astype(BF16)
    low = (a - high.astype(F32)).astype(BF16)
    return high, low


def left_operand(a):
    lane = iota(a.shape, 1)
    high = a.astype(BF16).astype(F32)
    low = a - high
    turned = pltpu.roll(high, MEMBERS, 1)
    one = jnp.where(lane < MEMBERS, high, turned)
    two = jnp.where(lane < 32, turned, pltpu.roll(low, 32, 1))
    return jnp.concatenate([one, two], axis=1).astype(BF16)


def spot(a, j):
    return jnp.broadcast_to(a[j : j + 1, :], (8, 128))


def eliminated(groups):
    lane, sub = iota((8, 128), 1), iota((8, 128), 0)
    groups, finished = list(groups), []
    for b in range(10):
        base = 8 * b
        block = (lane >= base) & (lane < base + 8)
        columns = [
            [jnp.broadcast_to(groups[g][:, base + j : base + j + 1], (8, 128)) for j in range(8)]
            for g in range(b, 10)
        ]
        square = columns[0]
        here = jnp.where(block, jnp.where(lane - base == sub, 1.0, 0.0), groups[b])
        pivots, inverses = square[0], None
        square = list(square)
        for j in range(8):
            inverse = 1.0 / spot(square[j], j)
            pivots = jnp.where(sub == j, square[j], pivots)
            inverses = inverse if j == 0 else jnp.where(sub == j, inverse, inverses)
            if j < 7:
                factor = jnp.where(sub > j, square[j] * inverse, 0.0)
                for i in range(j + 1, 8):
                    square[i] = square[i] - factor * spot(square[i], j)
                here = here - factor * spot(here, j)
        finished.append(here * lax.rsqrt(pivots))
        if b == 9:
            break
        solved = here * inverses
        for j in range(7, 0, -1):
            solved = solved - jnp.where(sub < j, square[j] * inverses, 0.0) * spot(solved, j)
        rows = [spot(solved, j) for j in range(8)]
        for g in range(b + 1, 10):
            terms = [c * row for c, row in zip(columns[g - b], rows)]
            while len(terms) > 1:
                terms = [p + q for p, q in zip(terms[::2], terms[1::2])]
            groups[g] = jnp.where(block, 0.0, groups[g]) - terms[0]
    return finished


def transform_rows(system_ref):
    lane, sub = iota((8, 128), 1), iota((8, 128), 0)
    groups = [
        system_ref[8 * g : 8 * g + 8, :] + jnp.where(lane == sub + 8 * g, MEMBERS - 1.0, 0.0) for g in range(10)
    ]
    weights, mean = jnp.zeros((8, 128), F32), jnp.zeros((8, 128), F32)
    centered = []
    for g, rows in enumerate(eliminated(groups)):
        partial = jnp.broadcast_to(rows[:, MEMBERS : MEMBERS + 1], (8, 128))
        inverse = jnp.where(lane <= sub + 8 * g, rows, 0.0)
        average = jnp.broadcast_to(jnp.sum(inverse, axis=1, keepdims=True), (8, 128)) * (1.0 / MEMBERS)
        weights = weights + partial * inverse
        mean = mean + partial * average
        centered.append(math.sqrt(MEMBERS - 1.0) * (inverse - average))
    shift = jnp.sum(weights - mean, axis=0, keepdims=True) + 1.0 / MEMBERS
    return jnp.concatenate([jnp.where(lane < MEMBERS, c + shift, 0.0) for c in centered], axis=0)


def kernel(
    bg, cell_in, wgt_in, val_in, err_in, cnt_in, bat_in, out,
    cell, wgt, val, err, cnt, bat, bgv, x, xcat, halo, from_left, from_right, mine, priors, full, spread, parts, shares,
    own, zone, bslots, bfull, mixed, cslots, system, own2, zone2, mixed2, cslots2, system2,
    load_sem, bulk_s, bulk_r, halo_s, left_r, right_r, prior_s, prior_r, share_s, share_r,
    zone_s, zone_r, b_s, b_r, c_s, c_r, zone2_s, zone2_r, c2_s, c2_r,
):
    t, y, z = lax.axis_index("tile"), lax.axis_index("member"), lax.axis_index("region")
    core, q = rem(t, 2), 4 * y + lax.div(t, 2)

    def at(dt, dy, dz):
        return {
            "tile": rem(t + dt, TILES),
            "member": rem(y + dy, SPLIT),
            "region": rem(z + dz, REGIONS),
        }

    def push(src, dst, s, r, where):
        copy = pltpu.make_async_remote_copy(
            src_ref=src, dst_ref=dst, send_sem=s, recv_sem=r, device_id=where, device_id_type=MESH
        )
        return copy

    plane = [(dt, dy) for dy in range(SPLIT) for dt in range(TILES) if (dt, dy) != (0, 0)]
    peers = [(dt, dy, 0) for dt, dy in plane] + [(0, 0, dz) for dz in range(1, REGIONS)]

    load = pltpu.make_async_copy(bg, bgv, load_sem.at[0])
    load.start()
    small = ((cell_in, cell), (wgt_in, wgt), (val_in, val), (err_in, err), (cnt_in, cnt), (bat_in, bat))
    small = [pltpu.make_async_copy(src, dst, load_sem.at[2 + i]) for i, (src, dst) in enumerate(small)]
    for copy in small:
        copy.start()
    barrier = pltpu.get_barrier_semaphore()
    for dt, dy, dz in peers:
        pl.semaphore_signal(barrier, inc=1, device_id=at(dt, dy, dz), device_id_type=MESH)

    for copy in small:
        copy.wait()
    place = cell[...]
    at_row, at_col = lax.shift_right_logical(place, 10), place & 1023
    w = [wgt[k] for k in range(4)]
    step = iota((1024, 128), 0) - (at_col - 1)
    taps = jnp.where(step == 0, w[0], jnp.where(step == 1, w[1], jnp.where(step == 2, w[2], jnp.where(step == 3, w[3], 0.0))))
    filled = iota((1, 128), 1) < cnt[...]
    inverse_error = 1.0 / err[...]
    scales = [jnp.where(filled & (bat[...] == b), inverse_error, 0.0) for b in range(2)]
    load.wait()

    packed = jnp.zeros((8, 128), F32)
    lane8 = iota((8, 128), 1)
    for a in range(3):
        count = min(8, PART - 8 * a)
        for r in range(8):
            ends = [bgv[8 * a : 8 * a + count, r, c : c + 128] for c in (896, 0)]
            if count < 8:
                ends = [jnp.concatenate([e, jnp.zeros((8 - count, 128), F32)], axis=0) for e in ends]
            for j, (end, lane) in enumerate(((ends[0], 127), (ends[1], 0), (ends[1], 1))):
                target = 32 * a + 8 * j + r
                packed = jnp.where(lane8 == target, pltpu.roll(end, (target - lane) % 128, 1), packed)
    halo[...] = packed

    rows = bgv[...].reshape(PART * 8, 1024)
    taken = jnp.dot(rows, taps, precision=EXACT, preferred_element_type=F32).reshape(PART, 8, 128)
    chosen = iota((8, 128), 0) == at_row
    mine[...] = jnp.zeros_like(mine)
    mine[0:PART, :] = jnp.sum(jnp.where(chosen[None], taken, 0.0), axis=1)

    near = []
    for d in range(REGIONS):
        other = rem(z - d + REGIONS, REGIONS)
        distance = jnp.full((8, 128), z - other, jnp.int32).astype(F32) * (4.0 / REGIONS)
        near.append(jnp.exp(-0.5 * distance * distance))

    pl.semaphore_wait(barrier, len(peers))

    sent = []

    def go(copy):
        copy.start()
        sent.append(copy)

    for i in range(1, SPLIT):
        go(push(mine, priors.at[y], prior_s.at[i - 1], prior_r.at[y], at(0, i, 0)))
    for i in range(SPLIT):
        go(push(halo, from_left.at[y], halo_s.at[i], left_r.at[y], at(1, i, 0)))
        go(push(halo, from_right.at[y], halo_s.at[4 + i], right_r.at[y], at(TILES - 1, i, 0)))
    for i in range(1, SPLIT):
        to = rem(y + i, SPLIT)
        columns = pl.ds(pl.multiple_of(to * 256, 256), 256)
        go(push(bgv.at[:, :, columns], x.at[pl.ds(y * PART, PART)], bulk_s.at[i - 1], bulk_r.at[y], at(0, i, 0)))
    keep = pltpu.make_async_copy(
        bgv.at[:, :, pl.ds(pl.multiple_of(y * 256, 256), 256)], x.at[pl.ds(y * PART, PART)], load_sem.at[1]
    )
    keep.start()
    priors[y] = mine[...]

    v = [
        jnp.where((t > 0) & (at_col == 0), w[0], 0.0),
        jnp.where(t < TILES - 1, jnp.where(at_col == 1023, w[2], jnp.where(at_col == 1022, w[3], 0.0)), 0.0),
        jnp.where((t < TILES - 1) & (at_col == 1023), w[3], 0.0),
    ]
    block = jnp.concatenate([jnp.where(chosen, value, 0.0) for value in v] + [jnp.zeros((8, 128), F32)], axis=0)
    nothing = jnp.zeros((32, 128), F32)
    spots = jnp.concatenate(
        [jnp.concatenate([block if b == a else nothing for b in range(4)], axis=0) for a in range(3)], axis=1
    )
    for i in range(SPLIT):
        push(halo, from_left.at[i], halo_s.at[0], left_r.at[i], at(0, 0, 0)).wait_recv()
        push(halo, from_right.at[i], halo_s.at[0], right_r.at[i], at(0, 0, 0)).wait_recv()
    from_j0 = (lane8 & 31) < 8
    sides = jnp.concatenate([jnp.where(from_j0, from_left[i], from_right[i]) for i in range(SPLIT)], axis=0)
    extra = jnp.dot(sides, spots, precision=EXACT, preferred_element_type=F32)
    for i in range(1, SPLIT):
        it = rem(y + i, SPLIT)
        push(mine, priors.at[it], prior_s.at[0], prior_r.at[it], at(0, 0, 0)).wait_recv()
    for i in range(SPLIT):
        for a in range(3):
            full[PART * i + 8 * a : PART * i + 8 * a + 8, :] = (
                priors[i, 8 * a : 8 * a + 8, :] + extra[8 * i : 8 * i + 8, 128 * a : 128 * a + 128]
            )
    ensemble = full[0:MEMBERS, :]
    average = jnp.sum(ensemble, axis=0, keepdims=True) / MEMBERS
    spread[MEMBERS : 128, :] = jnp.where(iota((48, 128), 0) == 0, val[...] - average, 0.0)
    spread[0:MEMBERS, :] = ensemble - average
    picks = []
    for c in range(8):
        start = y * PART + 5 * (c // 2)
        picks.append(spread[pl.ds(start, 8), :] * scales[c % 2])
    products = lax.dot_general(
        jnp.concatenate(picks, axis=0), spread[...], NT, precision=EXACT, preferred_element_type=F32
    )
    for c in range(8):
        parts[c] = products[8 * c : 8 * c + 8, :]
    for d in range(1, TILES):
        to = rem(t + d, TILES)
        go(push(parts.at[to], shares.at[d - 1], share_s.at[d - 1], share_r.at[d - 1], at(d, 0, 0)))
    total = parts[t]
    for d in range(1, TILES):
        push(parts.at[0], shares.at[d - 1], share_s.at[0], share_r.at[d - 1], at(0, 0, 0)).wait_recv()
    for d in range(1, TILES):
        total = total + shares[d - 1]
    own[...] = total

    def to_plane(src, slots, s, r):
        return [push(src, slots.at[q], s.at[i], r.at[q], at(dt, dy, 0)) for i, (dt, dy) in enumerate(plane)]

    def to_zone(src, slots, s, r):
        return [push(src, slots.at[d - 1], s.at[d - 1], r.at[d - 1], at(0, 0, d)) for d in range(1, REGIONS)]

    def mix(src, slots, s, r):
        for d in range(1, REGIONS):
            push(src, slots.at[d - 1], s.at[0], r.at[d - 1], at(0, 0, 0)).wait_recv()
        result = near[0] * src[...]
        for d in range(1, REGIONS):
            result = result + near[d] * slots[d - 1]
        return result

    def gathered(src, slots, s, r, owner, whole):
        for p in range(16):
            @pl.when((core != owner) | (q != p))
            def _():
                push(src, slots.at[p], s.at[0], r.at[p], at(0, 0, 0)).wait_recv()
        for p in range(16):
            whole[5 * p : 5 * p + 8, :] = slots[p]

    b_copies = to_plane(own, bslots, b_s, b_r)
    z_copies = to_zone(own, zone, zone_s, zone_r)
    c_copies = to_plane(mixed, cslots, c_s, c_r)
    z2_copies = to_zone(own2, zone2, zone2_s, zone2_r)
    c2_copies = to_plane(mixed2, cslots2, c2_s, c2_r)

    @pl.when(core == 0)
    def _():
        for copy in z_copies:
            copy.start()
        mixed[...] = mix(own, zone, zone_s, zone_r)
        for copy in c_copies:
            copy.start()
        cslots[q] = mixed[...]

    @pl.when(core == 1)
    def _():
        for copy in b_copies:
            copy.start()
        bslots[q] = own[...]

    gathered(own, bslots, b_s, b_r, 1, bfull)
    bfull[MEMBERS : 128, :] = jnp.zeros((48, 128), F32)
    gathered(mixed, cslots, c_s, c_r, 0, system)
    first = transform_rows(system)

    lane, row = iota((MEMBERS, 128), 1), iota((MEMBERS, 128), 0)
    mean_row = jnp.sum(first, axis=0, keepdims=True) / MEMBERS
    system[0:MEMBERS, :] = first - mean_row
    left = jnp.dot(system[pl.ds(5 * q, 8), :], bfull[...], precision=EXACT, preferred_element_type=F32)
    right = jnp.concatenate(
        [system[0:MEMBERS, :], jnp.where(iota((48, 128), 0) == 0, mean_row, 0.0)], axis=0
    )
    stats = lax.dot_general(
        jnp.where(lane8 < MEMBERS, left, 0.0), right, NT, precision=EXACT, preferred_element_type=F32
    )
    own2[...] = jnp.where(lane8 == MEMBERS, left - stats, stats)

    @pl.when(core == 0)
    def _():
        for copy in z2_copies:
            copy.start()

    keep.wait()
    for i in range(1, SPLIT):
        it = rem(y + i, SPLIT)
        push(
            bgv.at[:, :, 0:256], x.at[pl.ds(it * PART, PART)], bulk_s.at[0], bulk_r.at[it], at(0, 0, 0)
        ).wait_recv()
    first_left = left_operand(first)
    blank = jnp.zeros((16, 256), BF16)
    for r in range(8):
        high, low = halves(x[:, r, :])
        middle = jnp.dot(first_left, jnp.concatenate([high, low, high, blank], axis=0), preferred_element_type=F32)
        high, low = halves(middle)
        xcat[r, 0:80, :] = high
        xcat[r, 80:160, :] = low
        xcat[r, 160:240, :] = high
        xcat[r, 240:256, :] = blank

    @pl.when(core == 0)
    def _():
        mixed2[...] = mix(own2, zone2, zone2_s, zone2_r)
        for copy in c2_copies:
            copy.start()
        cslots2[q] = mixed2[...]

    gathered(mixed2, cslots2, c2_s, c2_r, 0, system2)
    second_left = left_operand(transform_rows(system2))
    for r in range(8):
        out[:, r, :] = jnp.dot(second_left, xcat[r], preferred_element_type=F32)
    for copy in sent:
        copy.wait_send()

    @pl.when(core == 0)
    def _():
        for copy in z_copies + c_copies + z2_copies + c2_copies:
            copy.wait_send()

    @pl.when(core == 1)
    def _():
        for copy in b_copies:
            copy.wait_send()


def shards(background, obs_cell, obs_weight, obs_value, obs_error, obs_count, obs_batch):
    hbm = pl.BlockSpec(memory_space=pltpu.HBM)
    tile = (8, 128)
    dma = pltpu.SemaphoreType.DMA
    return pl.pallas_call(
        kernel,
        out_shape=jax.ShapeDtypeStruct((MEMBERS, 8, 256), F32),
        in_specs=[hbm] * 7,
        out_specs=pl.BlockSpec(memory_space=pltpu.VMEM),
        scratch_shapes=[
            pltpu.VMEM((1, 128), jnp.int32),
            pltpu.VMEM((4, 1, 128), F32),
            pltpu.VMEM((1, 128), F32),
            pltpu.VMEM((1, 128), F32),
            pltpu.VMEM((1, 1), jnp.int32),
            pltpu.VMEM((1, 128), jnp.int32),
            pltpu.VMEM((PART, 8, 1024), F32),
            pltpu.VMEM((MEMBERS, 8, 256), F32),
            pltpu.VMEM((8, 256, 256), BF16),
            pltpu.VMEM(tile, F32),
            pltpu.VMEM((SPLIT, *tile), F32),
            pltpu.VMEM((SPLIT, *tile), F32),
            pltpu.VMEM((24, 128), F32),
            pltpu.VMEM((SPLIT, 24, 128), F32),
            pltpu.VMEM((88, 128), F32),
            pltpu.VMEM((128, 128), F32),
            pltpu.VMEM((TILES, *tile), F32),
            pltpu.VMEM((TILES - 1, *tile), F32),
            pltpu.VMEM(tile, F32),
            pltpu.VMEM((REGIONS - 1, *tile), F32),
            pltpu.VMEM((16, *tile), F32),
            pltpu.VMEM((128, 128), F32),
            pltpu.VMEM(tile, F32),
            pltpu.VMEM((16, *tile), F32),
            pltpu.VMEM((88, 128), F32),
            pltpu.VMEM(tile, F32),
            pltpu.VMEM((REGIONS - 1, *tile), F32),
            pltpu.VMEM(tile, F32),
            pltpu.VMEM((16, *tile), F32),
            pltpu.VMEM((88, 128), F32),
            dma((8,)), dma((3,)), dma((4,)), dma((8,)), dma((4,)), dma((4,)), dma((3,)), dma((4,)),
            dma((7,)), dma((7,)), dma((15,)), dma((15,)), dma((31,)), dma((16,)), dma((31,)), dma((16,)),
            dma((15,)), dma((15,)), dma((31,)), dma((16,)),
        ],
        compiler_params=pltpu.CompilerParams(
            collective_id=0, has_side_effects=True, vmem_limit_bytes=67043328
        ),
    )(background, obs_cell, obs_weight, obs_value, obs_error, obs_count, obs_batch)


def solution(mesh):
    return jax.shard_map(
        shards,
        mesh=mesh,
        in_specs=(
            P("member", "region", "tile"),
            P("region", "tile"),
            P(None, "region", "tile"),
            P("region", "tile"),
            P("region", "tile"),
            P("region", "tile"),
            P("region", "tile"),
        ),
        out_specs=P(None, "region", ("tile", "member")),
        check_vma=False,
    )
```

```python
import functools
import math

import jax
import jax.numpy as jnp
from jax import lax
from jax.experimental import pallas as pl
from jax.experimental.pallas import tpu as pltpu
from jax.sharding import PartitionSpec as P

EXACT = lax.Precision.HIGHEST
MESH = pl.DeviceIdType.MESH
F32 = jnp.float32
BF16 = jnp.bfloat16
MEMBERS = 80
TILES, SPLIT, REGIONS = 8, 4, 16
PART = MEMBERS // SPLIT
NT = (((1,), (1,)), ((), ()))


def rem(a, n):
    return lax.rem(a, n)


def iota(shape, dim):
    return lax.broadcasted_iota(jnp.int32, shape, dim)


def halves(a):
    high = a.astype(BF16)
    low = (a - high.astype(F32)).astype(BF16)
    return high, low


def left_operand(a):
    lane = iota(a.shape, 1)
    high = a.astype(BF16).astype(F32)
    low = a - high
    turned = pltpu.roll(high, MEMBERS, 1)
    one = jnp.where(lane < MEMBERS, high, turned)
    two = jnp.where(lane < 32, turned, pltpu.roll(low, 32, 1))
    return jnp.concatenate([one, two], axis=1).astype(BF16)


def spot(a, j):
    return jnp.broadcast_to(a[j : j + 1, :], (8, 128))


def eliminated(groups):
    lane, sub = iota((8, 128), 1), iota((8, 128), 0)
    groups, finished = list(groups), []
    for b in range(10):
        base = 8 * b
        block = (lane >= base) & (lane < base + 8)
        columns = [
            [jnp.broadcast_to(groups[g][:, base + j : base + j + 1], (8, 128)) for j in range(8)]
            for g in range(b, 10)
        ]
        square = columns[0]
        here = jnp.where(block, jnp.where(lane - base == sub, 1.0, 0.0), groups[b])
        pivots, inverses = square[0], None
        square = list(square)
        for j in range(8):
            inverse = 1.0 / spot(square[j], j)
            pivots = jnp.where(sub == j, square[j], pivots)
            inverses = inverse if j == 0 else jnp.where(sub == j, inverse, inverses)
            if j < 7:
                factor = jnp.where(sub > j, square[j] * inverse, 0.0)
                for i in range(j + 1, 8):
                    square[i] = square[i] - factor * spot(square[i], j)
                here = here - factor * spot(here, j)
        finished.append(here * lax.rsqrt(pivots))
        if b == 9:
            break
        solved = here * inverses
        for j in range(7, 0, -1):
            solved = solved - jnp.where(sub < j, square[j] * inverses, 0.0) * spot(solved, j)
        rows = [spot(solved, j) for j in range(8)]
        for g in range(b + 1, 10):
            terms = [c * row for c, row in zip(columns[g - b], rows)]
            while len(terms) > 1:
                terms = [p + q for p, q in zip(terms[::2], terms[1::2])]
            groups[g] = jnp.where(block, 0.0, groups[g]) - terms[0]
    return finished


def transform_rows(system_ref):
    lane, sub = iota((8, 128), 1), iota((8, 128), 0)
    groups = [
        system_ref[8 * g : 8 * g + 8, :] + jnp.where(lane == sub + 8 * g, MEMBERS - 1.0, 0.0) for g in range(10)
    ]
    weights, mean = jnp.zeros((8, 128), F32), jnp.zeros((8, 128), F32)
    centered = []
    for g, rows in enumerate(eliminated(groups)):
        partial = jnp.broadcast_to(rows[:, MEMBERS : MEMBERS + 1], (8, 128))
        inverse = jnp.where(lane <= sub + 8 * g, rows, 0.0)
        average = jnp.broadcast_to(jnp.sum(inverse, axis=1, keepdims=True), (8, 128)) * (1.0 / MEMBERS)
        weights = weights + partial * inverse
        mean = mean + partial * average
        centered.append(math.sqrt(MEMBERS - 1.0) * (inverse - average))
    shift = jnp.sum(weights - mean, axis=0, keepdims=True) + 1.0 / MEMBERS
    return jnp.concatenate([jnp.where(lane < MEMBERS, c + shift, 0.0) for c in centered], axis=0)


def kernel(
    bg, cell_in, wgt_in, val_in, err_in, cnt, bat_in, out,
    cell, wgt, val, err, bat, bgv, x, xcat, halo, from_left, from_right, mine, priors, full, spread, parts, shares,
    own, zone, bslots, bfull, mixed, cslots, system, own2, zone2, mixed2, cslots2, system2,
    load_sem, bulk_s, bulk_r, halo_s, left_r, right_r, prior_s, prior_r, share_s, share_r,
    zone_s, zone_r, b_s, b_r, c_s, c_r, zone2_s, zone2_r, c2_s, c2_r, ring,
):
    t, y, z = lax.axis_index("tile"), lax.axis_index("member"), lax.axis_index("region")
    core, q = rem(t, 2), 4 * y + lax.div(t, 2)

    def at(dt, dy, dz):
        return {
            "tile": rem(t + dt, TILES),
            "member": rem(y + dy, SPLIT),
            "region": rem(z + dz, REGIONS),
        }

    def push(src, dst, s, r, where):
        copy = pltpu.make_async_remote_copy(
            src_ref=src, dst_ref=dst, send_sem=s, recv_sem=r, device_id=where, device_id_type=MESH
        )
        return copy

    plane = [(dt, dy) for dy in range(SPLIT) for dt in range(TILES) if (dt, dy) != (0, 0)]
    near_by = {(dt, 0, 0) for dt in range(1, TILES)} | {(0, dy, 0) for dy in range(1, SPLIT)}
    near_by |= {(dt, dy, 0) for dt in (1, TILES - 1) for dy in range(SPLIT)} | {(0, 0, 1), (0, 0, REGIONS - 1)}
    peers = sorted(near_by)

    load = pltpu.make_async_copy(bg, bgv, load_sem.at[0])
    load.start()
    small = ((cell_in, cell), (wgt_in, wgt), (val_in, val), (err_in, err), (bat_in, bat))
    small = [pltpu.make_async_copy(src, dst, load_sem.at[2 + i]) for i, (src, dst) in enumerate(small)]
    for copy in small:
        copy.start()
    barrier = pltpu.get_barrier_semaphore()
    for dt, dy, dz in peers:
        pl.semaphore_signal(barrier, inc=1, device_id=at(dt, dy, dz), device_id_type=MESH)

    for copy in small:
        copy.wait()
    place = cell[...]
    at_row, at_col = lax.shift_right_logical(place, 10), place & 1023
    w = [wgt[k] for k in range(4)]
    step = iota((1024, 128), 0) - (at_col - 1)
    taps = jnp.where(step == 0, w[0], jnp.where(step == 1, w[1], jnp.where(step == 2, w[2], jnp.where(step == 3, w[3], 0.0))))
    filled = iota((1, 128), 1) < cnt[0, 0]
    inverse_error = 1.0 / err[...]
    scales = [jnp.where(filled & (bat[...] == b), inverse_error, 0.0) for b in range(2)]
    load.wait()

    packed = jnp.zeros((8, 128), F32)
    lane8 = iota((8, 128), 1)
    for a in range(3):
        count = min(8, PART - 8 * a)
        for r in range(8):
            ends = [bgv[8 * a : 8 * a + count, r, c : c + 128] for c in (896, 0)]
            if count < 8:
                ends = [jnp.concatenate([e, jnp.zeros((8 - count, 128), F32)], axis=0) for e in ends]
            for j, (end, lane) in enumerate(((ends[0], 127), (ends[1], 0), (ends[1], 1))):
                target = 32 * a + 8 * j + r
                packed = jnp.where(lane8 == target, pltpu.roll(end, (target - lane) % 128, 1), packed)
    halo[...] = packed

    rows = bgv[...].reshape(PART * 8, 1024)
    taken = jnp.dot(rows, taps, precision=EXACT, preferred_element_type=F32).reshape(PART, 8, 128)
    chosen = iota((8, 128), 0) == at_row
    mine[...] = jnp.zeros_like(mine)
    mine[0:PART, :] = jnp.sum(jnp.where(chosen[None], taken, 0.0), axis=1)

    near = []
    for d in range(REGIONS):
        other = rem(z - d + REGIONS, REGIONS)
        distance = jnp.full((8, 128), z - other, jnp.int32).astype(F32) * (4.0 / REGIONS)
        near.append(jnp.exp(-0.5 * distance * distance))

    pl.semaphore_wait(barrier, len(peers))

    def tell(step):
        @pl.when(core == 0)
        def _():
            for dz in (1 << step, REGIONS - (1 << step)):
                pl.semaphore_signal(ring.at[step], inc=1, device_id=at(0, 0, dz), device_id_type=MESH)

    def heard(step):
        @pl.when(core == 0)
        def _():
            pl.semaphore_wait(ring.at[step], 2)

    tell(0)
    sent = []

    def go(copy):
        copy.start()
        sent.append(copy)

    for i in range(1, SPLIT):
        go(push(mine, priors.at[y], prior_s.at[i - 1], prior_r.at[y], at(0, i, 0)))
    for i in range(SPLIT):
        go(push(halo, from_left.at[y], halo_s.at[i], left_r.at[y], at(1, i, 0)))
        go(push(halo, from_right.at[y], halo_s.at[4 + i], right_r.at[y], at(TILES - 1, i, 0)))
    priors[y] = mine[...]

    v = [
        jnp.where((t > 0) & (at_col == 0), w[0], 0.0),
        jnp.where(t < TILES - 1, jnp.where(at_col == 1023, w[2], jnp.where(at_col == 1022, w[3], 0.0)), 0.0),
        jnp.where((t < TILES - 1) & (at_col == 1023), w[3], 0.0),
    ]
    block = jnp.concatenate([jnp.where(chosen, value, 0.0) for value in v] + [jnp.zeros((8, 128), F32)], axis=0)
    nothing = jnp.zeros((32, 128), F32)
    spots = jnp.concatenate(
        [jnp.concatenate([block if b == a else nothing for b in range(4)], axis=0) for a in range(3)], axis=1
    )
    heard(0)
    tell(1)
    for i in range(SPLIT):
        push(halo, from_left.at[i], halo_s.at[0], left_r.at[i], at(0, 0, 0)).wait_recv()
        push(halo, from_right.at[i], halo_s.at[0], right_r.at[i], at(0, 0, 0)).wait_recv()
    from_j0 = (lane8 & 31) < 8
    sides = jnp.concatenate([jnp.where(from_j0, from_left[i], from_right[i]) for i in range(SPLIT)], axis=0)
    extra = jnp.dot(sides, spots, precision=EXACT, preferred_element_type=F32)
    for i in range(1, SPLIT):
        it = rem(y + i, SPLIT)
        push(mine, priors.at[it], prior_s.at[0], prior_r.at[it], at(0, 0, 0)).wait_recv()
    heard(1)
    tell(2)
    for i in range(SPLIT):
        for a in range(3):
            full[PART * i + 8 * a : PART * i + 8 * a + 8, :] = (
                priors[i, 8 * a : 8 * a + 8, :] + extra[8 * i : 8 * i + 8, 128 * a : 128 * a + 128]
            )
    ensemble = full[0:MEMBERS, :]
    average = jnp.sum(ensemble, axis=0, keepdims=True) / MEMBERS
    spread[MEMBERS : 128, :] = jnp.where(iota((48, 128), 0) == 0, val[...] - average, 0.0)
    spread[0:MEMBERS, :] = ensemble - average
    picks = []
    for c in range(8):
        start = y * PART + 5 * (c // 2)
        picks.append(spread[pl.ds(start, 8), :] * scales[c % 2])
    products = lax.dot_general(
        jnp.concatenate(picks, axis=0), spread[...], NT, precision=EXACT, preferred_element_type=F32
    )
    for c in range(8):
        parts[c] = products[8 * c : 8 * c + 8, :]
    for d in range(1, TILES):
        to = rem(t + d, TILES)
        go(push(parts.at[to], shares.at[d - 1], share_s.at[d - 1], share_r.at[d - 1], at(d, 0, 0)))
    for i in range(1, SPLIT):
        to = rem(y + i, SPLIT)
        columns = pl.ds(pl.multiple_of(to * 256, 256), 256)
        go(push(bgv.at[:, :, columns], x.at[pl.ds(y * PART, PART)], bulk_s.at[i - 1], bulk_r.at[y], at(0, i, 0)))
    keep = pltpu.make_async_copy(
        bgv.at[:, :, pl.ds(pl.multiple_of(y * 256, 256), 256)], x.at[pl.ds(y * PART, PART)], load_sem.at[1]
    )
    keep.start()
    total = parts[t]
    for d in range(1, TILES):
        push(parts.at[0], shares.at[d - 1], share_s.at[0], share_r.at[d - 1], at(0, 0, 0)).wait_recv()
    for d in range(1, TILES):
        total = total + shares[d - 1]
    own[...] = total

    def to_plane(src, slots, s, r):
        return [push(src, slots.at[q], s.at[i], r.at[q], at(dt, dy, 0)) for i, (dt, dy) in enumerate(plane)]

    def to_zone(src, slots, s, r):
        return [push(src, slots.at[d - 1], s.at[d - 1], r.at[d - 1], at(0, 0, d)) for d in range(1, REGIONS)]

    def mix(src, slots, s, r):
        for d in range(1, REGIONS):
            push(src, slots.at[d - 1], s.at[0], r.at[d - 1], at(0, 0, 0)).wait_recv()
        result = near[0] * src[...]
        for d in range(1, REGIONS):
            result = result + near[d] * slots[d - 1]
        return result

    def gathered(src, slots, s, r, owner, whole):
        for p in range(16):
            @pl.when((core != owner) | (q != p))
            def _():
                push(src, slots.at[p], s.at[0], r.at[p], at(0, 0, 0)).wait_recv()
        for p in range(16):
            whole[5 * p : 5 * p + 8, :] = slots[p]

    b_copies = to_plane(own, bslots, b_s, b_r)
    z_copies = to_zone(own, zone, zone_s, zone_r)
    c_copies = to_plane(mixed, cslots, c_s, c_r)
    z2_copies = to_zone(own2, zone2, zone2_s, zone2_r)
    c2_copies = to_plane(mixed2, cslots2, c2_s, c2_r)

    @pl.when(core == 0)
    def _():
        pl.semaphore_wait(ring.at[2], 2)
        for copy in z_copies:
            copy.start()
        mixed[...] = mix(own, zone, zone_s, zone_r)
        for copy in c_copies:
            copy.start()
        cslots[q] = mixed[...]

    @pl.when(core == 1)
    def _():
        for copy in b_copies:
            copy.start()
        bslots[q] = own[...]

    gathered(own, bslots, b_s, b_r, 1, bfull)
    bfull[MEMBERS : 128, :] = jnp.zeros((48, 128), F32)
    gathered(mixed, cslots, c_s, c_r, 0, system)
    first = transform_rows(system)

    lane, row = iota((MEMBERS, 128), 1), iota((MEMBERS, 128), 0)
    mean_row = jnp.sum(first, axis=0, keepdims=True) / MEMBERS
    system[0:MEMBERS, :] = first - mean_row
    left = jnp.dot(system[pl.ds(5 * q, 8), :], bfull[...], precision=EXACT, preferred_element_type=F32)
    right = jnp.concatenate(
        [system[0:MEMBERS, :], jnp.where(iota((48, 128), 0) == 0, mean_row, 0.0)], axis=0
    )
    stats = lax.dot_general(
        jnp.where(lane8 < MEMBERS, left, 0.0), right, NT, precision=EXACT, preferred_element_type=F32
    )
    own2[...] = jnp.where(lane8 == MEMBERS, left - stats, stats)

    @pl.when(core == 0)
    def _():
        for copy in z2_copies:
            copy.start()

    keep.wait()
    for i in range(1, SPLIT):
        it = rem(y + i, SPLIT)
        push(
            bgv.at[:, :, 0:256], x.at[pl.ds(it * PART, PART)], bulk_s.at[0], bulk_r.at[it], at(0, 0, 0)
        ).wait_recv()
    first_left = left_operand(first)
    blank = jnp.zeros((16, 256), BF16)
    for r in range(8):
        high, low = halves(x[:, r, :])
        middle = jnp.dot(first_left, jnp.concatenate([high, low, high, blank], axis=0), preferred_element_type=F32)
        high, low = halves(middle)
        xcat[r, 0:80, :] = high
        xcat[r, 80:160, :] = low
        xcat[r, 160:240, :] = high
        xcat[r, 240:256, :] = blank

    @pl.when(core == 0)
    def _():
        mixed2[...] = mix(own2, zone2, zone2_s, zone2_r)
        for copy in c2_copies:
            copy.start()
        cslots2[q] = mixed2[...]

    gathered(mixed2, cslots2, c2_s, c2_r, 0, system2)
    second_left = left_operand(transform_rows(system2))
    for r in range(8):
        out[:, r, :] = jnp.dot(second_left, xcat[r], preferred_element_type=F32)
    for copy in sent:
        copy.wait_send()

    @pl.when(core == 0)
    def _():
        for copy in z_copies + c_copies + z2_copies + c2_copies:
            copy.wait_send()

    @pl.when(core == 1)
    def _():
        for copy in b_copies:
            copy.wait_send()


def shards(*operands):
    hbm = pl.BlockSpec(memory_space=pltpu.HBM)
    tile = (8, 128)
    dma = pltpu.SemaphoreType.DMA
    return pl.pallas_call(
        kernel,
        out_shape=jax.ShapeDtypeStruct((MEMBERS, 8, 256), F32),
        in_specs=[hbm] * 5 + [pl.BlockSpec(memory_space=pltpu.SMEM), hbm],
        out_specs=pl.BlockSpec(memory_space=pltpu.VMEM),
        scratch_shapes=[
            pltpu.VMEM((1, 128), jnp.int32),
            pltpu.VMEM((4, 1, 128), F32),
            pltpu.VMEM((1, 128), F32),
            pltpu.VMEM((1, 128), F32),
            pltpu.VMEM((1, 128), jnp.int32),
            pltpu.VMEM((PART, 8, 1024), F32),
            pltpu.VMEM((MEMBERS, 8, 256), F32),
            pltpu.VMEM((8, 256, 256), BF16),
            pltpu.VMEM(tile, F32),
            pltpu.VMEM((SPLIT, *tile), F32),
            pltpu.VMEM((SPLIT, *tile), F32),
            pltpu.VMEM((24, 128), F32),
            pltpu.VMEM((SPLIT, 24, 128), F32),
            pltpu.VMEM((88, 128), F32),
            pltpu.VMEM((128, 128), F32),
            pltpu.VMEM((TILES, *tile), F32),
            pltpu.VMEM((TILES - 1, *tile), F32),
            pltpu.VMEM(tile, F32),
            pltpu.VMEM((REGIONS - 1, *tile), F32),
            pltpu.VMEM((16, *tile), F32),
            pltpu.VMEM((128, 128), F32),
            pltpu.VMEM(tile, F32),
            pltpu.VMEM((16, *tile), F32),
            pltpu.VMEM((88, 128), F32),
            pltpu.VMEM(tile, F32),
            pltpu.VMEM((REGIONS - 1, *tile), F32),
            pltpu.VMEM(tile, F32),
            pltpu.VMEM((16, *tile), F32),
            pltpu.VMEM((88, 128), F32),
            dma((7,)), dma((3,)), dma((4,)), dma((8,)), dma((4,)), dma((4,)), dma((3,)), dma((4,)),
            dma((7,)), dma((7,)), dma((15,)), dma((15,)), dma((31,)), dma((16,)), dma((31,)), dma((16,)),
            dma((15,)), dma((15,)), dma((31,)), dma((16,)), pltpu.SemaphoreType.REGULAR((3,)),
        ],
        compiler_params=pltpu.CompilerParams(
            collective_id=0, has_side_effects=True, vmem_limit_bytes=48 * 1024 * 1024
        ),
    )(*(a if i == 5 else pltpu.with_memory_space_constraint(a, pltpu.HBM) for i, a in enumerate(operands)))


def solution(mesh):
    return jax.shard_map(
        shards,
        mesh=mesh,
        in_specs=(
            P("member", "region", "tile"),
            P("region", "tile"),
            P(None, "region", "tile"),
            P("region", "tile"),
            P("region", "tile"),
            P("region", "tile"),
            P("region", "tile"),
        ),
        out_specs=P(None, "region", ("tile", "member")),
        check_vma=False,
    )
```

```python
import functools
import math

import jax
import jax.numpy as jnp
from jax import lax
from jax.experimental import pallas as pl
from jax.experimental.pallas import tpu as pltpu
from jax.sharding import PartitionSpec as P

EXACT = lax.Precision.HIGHEST
MESH = pl.DeviceIdType.MESH
F32 = jnp.float32
BF16 = jnp.bfloat16
MEMBERS = 80
TILES, SPLIT, REGIONS = 8, 4, 16
PART = MEMBERS // SPLIT
NT = (((1,), (1,)), ((), ()))


def rem(a, n):
    return lax.rem(a, n)


def iota(shape, dim):
    return lax.broadcasted_iota(jnp.int32, shape, dim)


def halves(a):
    high = a.astype(BF16)
    low = (a - high.astype(F32)).astype(BF16)
    return high, low


def left_operand(a):
    lane = iota(a.shape, 1)
    high = a.astype(BF16).astype(F32)
    low = a - high
    turned = pltpu.roll(high, MEMBERS, 1)
    one = jnp.where(lane < MEMBERS, high, turned)
    two = jnp.where(lane < 32, turned, pltpu.roll(low, 32, 1))
    return jnp.concatenate([one, two], axis=1).astype(BF16)


def spot(a, j):
    return jnp.broadcast_to(a[j : j + 1, :], (8, 128))


def eliminated(groups):
    lane, sub = iota((8, 128), 1), iota((8, 128), 0)
    groups, finished = list(groups), []
    for b in range(10):
        base = 8 * b
        block = (lane >= base) & (lane < base + 8)
        columns = [
            [jnp.broadcast_to(groups[g][:, base + j : base + j + 1], (8, 128)) for j in range(8)]
            for g in range(b, 10)
        ]
        square = columns[0]
        here = jnp.where(block, jnp.where(lane - base == sub, 1.0, 0.0), groups[b])
        pivots, inverses = square[0], None
        square = list(square)
        for j in range(8):
            inverse = 1.0 / spot(square[j], j)
            pivots = jnp.where(sub == j, square[j], pivots)
            inverses = inverse if j == 0 else jnp.where(sub == j, inverse, inverses)
            if j < 7:
                factor = jnp.where(sub > j, square[j] * inverse, 0.0)
                for i in range(j + 1, 8):
                    square[i] = square[i] - factor * spot(square[i], j)
                here = here - factor * spot(here, j)
        finished.append(here * lax.rsqrt(pivots))
        if b == 9:
            break
        solved = here * inverses
        for j in range(7, 0, -1):
            solved = solved - jnp.where(sub < j, square[j] * inverses, 0.0) * spot(solved, j)
        rows = [spot(solved, j) for j in range(8)]
        for g in range(b + 1, 10):
            terms = [c * row for c, row in zip(columns[g - b], rows)]
            while len(terms) > 1:
                terms = [p + q for p, q in zip(terms[::2], terms[1::2])]
            groups[g] = jnp.where(block, 0.0, groups[g]) - terms[0]
    return finished


def transform_rows(system_ref):
    lane, sub = iota((8, 128), 1), iota((8, 128), 0)
    groups = [
        system_ref[8 * g : 8 * g + 8, :] + jnp.where(lane == sub + 8 * g, MEMBERS - 1.0, 0.0) for g in range(10)
    ]
    weights, mean = jnp.zeros((8, 128), F32), jnp.zeros((8, 128), F32)
    centered = []
    for g, rows in enumerate(eliminated(groups)):
        partial = jnp.broadcast_to(rows[:, MEMBERS : MEMBERS + 1], (8, 128))
        inverse = jnp.where(lane <= sub + 8 * g, rows, 0.0)
        average = jnp.broadcast_to(jnp.sum(inverse, axis=1, keepdims=True), (8, 128)) * (1.0 / MEMBERS)
        weights = weights + partial * inverse
        mean = mean + partial * average
        centered.append(math.sqrt(MEMBERS - 1.0) * (inverse - average))
    shift = jnp.sum(weights - mean, axis=0, keepdims=True) + 1.0 / MEMBERS
    return jnp.concatenate([jnp.where(lane < MEMBERS, c + shift, 0.0) for c in centered], axis=0)


def kernel(
    bg, cell_in, wgt_in, val_in, err_in, cnt, bat_in, second, xout,
    cell, wgt, val, err, bat, bgv, x, xcat, halo, from_left, from_right, mine, priors, full, spread, parts, shares,
    own, zone, bslots, bfull, mixed, cslots, system, own2, zone2, mixed2, cslots2, system2,
    load_sem, bulk_s, bulk_r, halo_s, left_r, right_r, prior_s, prior_r, share_s, share_r,
    zone_s, zone_r, b_s, b_r, c_s, c_r, zone2_s, zone2_r, c2_s, c2_r, ring,
):
    t, y, z = lax.axis_index("tile"), lax.axis_index("member"), lax.axis_index("region")
    core, q = rem(t, 2), 4 * y + lax.div(t, 2)

    def at(dt, dy, dz):
        return {
            "tile": rem(t + dt, TILES),
            "member": rem(y + dy, SPLIT),
            "region": rem(z + dz, REGIONS),
        }

    def push(src, dst, s, r, where):
        copy = pltpu.make_async_remote_copy(
            src_ref=src, dst_ref=dst, send_sem=s, recv_sem=r, device_id=where, device_id_type=MESH
        )
        return copy

    plane = [(dt, dy) for dy in range(SPLIT) for dt in range(TILES) if (dt, dy) != (0, 0)]
    near_by = {(dt, 0, 0) for dt in range(1, TILES)} | {(0, dy, 0) for dy in range(1, SPLIT)}
    near_by |= {(dt, dy, 0) for dt in (1, TILES - 1) for dy in range(SPLIT)} | {(0, 0, dz) for dz in (1, 2, 3, 13, 14, 15)}
    plane.sort(key=lambda p: -(min((p[0] + 1) // 2, (TILES - p[0] + 1) // 2) + min(p[1], SPLIT - p[1])))
    peers = sorted(near_by)

    load = pltpu.make_async_copy(bg, bgv, load_sem.at[0])
    load.start()
    small = ((cell_in, cell), (wgt_in, wgt), (val_in, val), (err_in, err), (bat_in, bat))
    small = [pltpu.make_async_copy(src, dst, load_sem.at[2 + i]) for i, (src, dst) in enumerate(small)]
    for copy in small:
        copy.start()
    barrier = pltpu.get_barrier_semaphore()
    for dt, dy, dz in peers:
        pl.semaphore_signal(barrier, inc=1, device_id=at(dt, dy, dz), device_id_type=MESH)

    for copy in small:
        copy.wait()
    place = cell[...]
    at_row, at_col = lax.shift_right_logical(place, 10), place & 1023
    w = [wgt[k] for k in range(4)]
    step = iota((1024, 128), 0) - (at_col - 1)
    taps = jnp.where(step == 0, w[0], jnp.where(step == 1, w[1], jnp.where(step == 2, w[2], jnp.where(step == 3, w[3], 0.0))))
    filled = iota((1, 128), 1) < cnt[0, 0]
    inverse_error = 1.0 / err[...]
    scales = [jnp.where(filled & (bat[...] == b), inverse_error, 0.0) for b in range(2)]
    load.wait()

    packed = jnp.zeros((8, 128), F32)
    lane8 = iota((8, 128), 1)
    for a in range(3):
        count = min(8, PART - 8 * a)
        for r in range(8):
            ends = [bgv[8 * a : 8 * a + count, r, c : c + 128] for c in (896, 0)]
            if count < 8:
                ends = [jnp.concatenate([e, jnp.zeros((8 - count, 128), F32)], axis=0) for e in ends]
            for j, (end, lane) in enumerate(((ends[0], 127), (ends[1], 0), (ends[1], 1))):
                target = 32 * a + 8 * j + r
                packed = jnp.where(lane8 == target, pltpu.roll(end, (target - lane) % 128, 1), packed)
    halo[...] = packed

    rows = bgv[...].reshape(PART * 8, 1024)
    taken = jnp.dot(rows, taps, precision=EXACT, preferred_element_type=F32).reshape(PART, 8, 128)
    chosen = iota((8, 128), 0) == at_row
    mine[...] = jnp.zeros_like(mine)
    mine[0:PART, :] = jnp.sum(jnp.where(chosen[None], taken, 0.0), axis=1)

    near = []
    for d in range(REGIONS):
        other = rem(z - d + REGIONS, REGIONS)
        distance = jnp.full((5, 128), z - other, jnp.int32).astype(F32) * (4.0 / REGIONS)
        near.append(jnp.exp(-0.5 * distance * distance))

    pl.semaphore_wait(barrier, len(peers))

    def tell(step):
        @pl.when(core == 0)
        def _():
            for dz in (3 - step, REGIONS - 3 + step):
                pl.semaphore_signal(ring.at[step], inc=1, device_id=at(0, 0, dz), device_id_type=MESH)

    def heard(step):
        @pl.when(core == 0)
        def _():
            pl.semaphore_wait(ring.at[step], 2)

    tell(0)
    def arrived(like, semaphore):
        pltpu.make_async_copy(like, like, semaphore).wait()

    def go(copy):
        copy.start()

    for i in (2, 1, 3, 0):
        go(push(halo, from_left.at[y], halo_s, left_r, at(1, i, 0)))
        go(push(halo, from_right.at[y], halo_s, right_r, at(TILES - 1, i, 0)))
    for i in range(1, SPLIT):
        go(push(mine, priors.at[y], prior_s, prior_r, at(0, i, 0)))
    priors[y] = mine[...]

    v = [
        jnp.where((t > 0) & (at_col == 0), w[0], 0.0),
        jnp.where(t < TILES - 1, jnp.where(at_col == 1023, w[2], jnp.where(at_col == 1022, w[3], 0.0)), 0.0),
        jnp.where((t < TILES - 1) & (at_col == 1023), w[3], 0.0),
    ]
    block = jnp.concatenate([jnp.where(chosen, value, 0.0) for value in v] + [jnp.zeros((8, 128), F32)], axis=0)
    nothing = jnp.zeros((32, 128), F32)
    spots = jnp.concatenate(
        [jnp.concatenate([block if b == a else nothing for b in range(4)], axis=0) for a in range(3)], axis=1
    )
    heard(0)
    tell(1)
    arrived(from_left, left_r)
    arrived(from_right, right_r)
    from_j0 = (lane8 & 31) < 8
    sides = jnp.concatenate([jnp.where(from_j0, from_left[i], from_right[i]) for i in range(SPLIT)], axis=0)
    extra = jnp.dot(sides, spots, precision=EXACT, preferred_element_type=F32)
    arrived(priors.at[0 : SPLIT - 1], prior_r)
    for i in range(SPLIT):
        for a in range(3):
            full[PART * i + 8 * a : PART * i + 8 * a + 8, :] = (
                priors[i, 8 * a : 8 * a + 8, :] + extra[8 * i : 8 * i + 8, 128 * a : 128 * a + 128]
            )
    ensemble = full[0:MEMBERS, :]
    average = jnp.sum(ensemble, axis=0, keepdims=True) / MEMBERS
    spread[MEMBERS : 128, :] = jnp.where(iota((48, 128), 0) == 0, val[...] - average, 0.0)
    spread[0:MEMBERS, :] = ensemble - average
    picks = []
    for c in range(8):
        start = y * PART + 5 * (c // 2)
        picks.append(spread[pl.ds(start, 8), :] * scales[c % 2])
    products = lax.dot_general(
        jnp.concatenate(picks, axis=0), spread[...], NT, precision=EXACT, preferred_element_type=F32
    )
    for c in range(8):
        parts[c] = products[8 * c : 8 * c + 5, :]
    for d in range(1, TILES):
        to = rem(t + d, TILES)
        go(push(parts.at[to], shares.at[d - 1], share_s, share_r, at(d, 0, 0)))
    for i in range(1, SPLIT):
        to = rem(y + i, SPLIT)
        columns = pl.ds(pl.multiple_of(to * 256, 256), 256)
        go(push(bgv.at[:, :, columns], x.at[pl.ds(y * PART, PART)], bulk_s, bulk_r, at(0, i, 0)))
    keep = pltpu.make_async_copy(
        bgv.at[:, :, pl.ds(pl.multiple_of(y * 256, 256), 256)], x.at[pl.ds(y * PART, PART)], load_sem.at[1]
    )
    keep.start()
    total = parts[t]
    arrived(shares, share_r)
    for d in range(1, TILES):
        total = total + shares[d - 1]
    own[...] = total

    def to_plane(src, slots, s, r):
        return [push(src, slots.at[q], s, r, at(dt, dy, 0)) for dt, dy in plane]

    def to_zone(src, slots, s, r):
        return [push(src, slots.at[d - 1], s, r, at(0, 0, d)) for d in sorted(range(1, REGIONS), key=lambda d: -min(d, REGIONS - d))]

    def mix(src, slots, s, r):
        arrived(slots, r)
        result = near[0] * src[...]
        for d in range(1, REGIONS):
            result = result + near[d] * slots[d - 1]
        return result

    def gathered(src, slots, s, r, owner, whole):
        pl.when(core == owner)(lambda: arrived(slots.at[0:15], r))
        pl.when(core != owner)(lambda: arrived(slots, r))
        for p in range(16):
            whole[5 * p : 5 * p + 5, :] = slots[p]

    b_copies = to_plane(own, bslots, b_s, b_r)
    z_copies = to_zone(own, zone, zone_s, zone_r)
    c_copies = to_plane(mixed, cslots, c_s, c_r)
    z2_copies = to_zone(own2, zone2, zone2_s, zone2_r)
    c2_copies = to_plane(mixed2, cslots2, c2_s, c2_r)

    @pl.when(core == 0)
    def _():
        pl.semaphore_wait(ring.at[1], 2)
        for copy in z_copies:
            copy.start()
        mixed[...] = mix(own, zone, zone_s, zone_r)
        for copy in c_copies:
            copy.start()
        cslots[q] = mixed[...]

    @pl.when(core == 1)
    def _():
        for copy in b_copies:
            copy.start()
        bslots[q] = own[...]

    gathered(own, bslots, b_s, b_r, 1, bfull)
    bfull[MEMBERS : 128, :] = jnp.zeros((48, 128), F32)
    gathered(mixed, cslots, c_s, c_r, 0, system)
    first = transform_rows(system)

    lane, row = iota((MEMBERS, 128), 1), iota((MEMBERS, 128), 0)
    mean_row = jnp.sum(first, axis=0, keepdims=True) / MEMBERS
    system[0:MEMBERS, :] = first - mean_row
    left = jnp.dot(system[pl.ds(5 * q, 8), :], bfull[...], precision=EXACT, preferred_element_type=F32)
    right = jnp.concatenate(
        [system[0:MEMBERS, :], jnp.where(iota((48, 128), 0) == 0, mean_row, 0.0)], axis=0
    )
    stats = lax.dot_general(
        jnp.where(lane8 < MEMBERS, left, 0.0), right, NT, precision=EXACT, preferred_element_type=F32
    )
    own2[...] = jnp.where(lane8 == MEMBERS, left - stats, stats)[0:5, :]

    @pl.when(core == 0)
    def _():
        for copy in z2_copies:
            copy.start()

    @pl.when(core == 0)
    def _():
        mixed2[...] = mix(own2, zone2, zone2_s, zone2_r)
        for copy in c2_copies:
            copy.start()
        cslots2[q] = mixed2[...]

    keep.wait()
    arrived(x.at[0 : (SPLIT - 1) * PART], bulk_r)
    first_left = left_operand(first)
    blank = jnp.zeros((16, 256), BF16)
    for r in range(8):
        high, low = halves(x[:, r, :])
        middle = jnp.dot(first_left, jnp.concatenate([high, low, high, blank], axis=0), preferred_element_type=F32)
        high, low = halves(middle)
        xcat[r, 0:80, :] = high
        xcat[r, 80:160, :] = low
        xcat[r, 160:240, :] = high
        xcat[r, 240:256, :] = blank
    save = pltpu.make_async_copy(xcat, xout, load_sem.at[7])
    save.start()

    gathered(mixed2, cslots2, c2_s, c2_r, 0, system2)
    second[...] = left_operand(transform_rows(system2))
    save.wait()
    arrived(from_left, halo_s)
    arrived(from_right, halo_s)
    arrived(priors.at[0 : SPLIT - 1], prior_s)
    arrived(x.at[0 : (SPLIT - 1) * PART], bulk_s)
    arrived(shares, share_s)

    @pl.when(core == 0)
    def _():
        arrived(zone, zone_s)
        arrived(zone2, zone2_s)
        for semaphore in (c_s, c2_s):
            arrived(cslots, semaphore)
            arrived(cslots.at[0:15], semaphore)

    @pl.when(core == 1)
    def _():
        arrived(bslots, b_s)
        arrived(bslots.at[0:15], b_s)


def product(second, middle, out):
    for r in range(8):
        out[:, r, :] = jnp.dot(second[...], middle[r], preferred_element_type=F32)


def shards(*operands):
    vmem = pl.BlockSpec(memory_space=pltpu.VMEM)
    hbm = pl.BlockSpec(memory_space=pltpu.HBM)
    tile = (8, 128)
    short = (5, 128)
    dma = pltpu.SemaphoreType.DMA
    second, middle = pl.pallas_call(
        kernel,
        out_shape=(jax.ShapeDtypeStruct((MEMBERS, 256), BF16), jax.ShapeDtypeStruct((8, 256, 256), BF16)),
        in_specs=[hbm] * 5 + [pl.BlockSpec(memory_space=pltpu.SMEM), hbm],
        out_specs=(vmem, pl.BlockSpec(memory_space=pl.ANY)),
        scratch_shapes=[
            pltpu.VMEM((1, 128), jnp.int32),
            pltpu.VMEM((4, 1, 128), F32),
            pltpu.VMEM((1, 128), F32),
            pltpu.VMEM((1, 128), F32),
            pltpu.VMEM((1, 128), jnp.int32),
            pltpu.VMEM((PART, 8, 1024), F32),
            pltpu.VMEM((MEMBERS, 8, 256), F32),
            pltpu.VMEM((8, 256, 256), BF16),
            pltpu.VMEM(tile, F32),
            pltpu.VMEM((SPLIT, *tile), F32),
            pltpu.VMEM((SPLIT, *tile), F32),
            pltpu.VMEM((24, 128), F32),
            pltpu.VMEM((SPLIT, 24, 128), F32),
            pltpu.VMEM((88, 128), F32),
            pltpu.VMEM((128, 128), F32),
            pltpu.VMEM((TILES, *short), F32),
            pltpu.VMEM((TILES - 1, *short), F32),
            pltpu.VMEM(short, F32),
            pltpu.VMEM((REGIONS - 1, *short), F32),
            pltpu.VMEM((16, *short), F32),
            pltpu.VMEM((128, 128), F32),
            pltpu.VMEM(short, F32),
            pltpu.VMEM((16, *short), F32),
            pltpu.VMEM((88, 128), F32),
            pltpu.VMEM(short, F32),
            pltpu.VMEM((REGIONS - 1, *short), F32),
            pltpu.VMEM(short, F32),
            pltpu.VMEM((16, *short), F32),
            pltpu.VMEM((88, 128), F32),
            dma((8,)),
            *[dma] * 19,
            pltpu.SemaphoreType.REGULAR((2,)),
        ],
        compiler_params=pltpu.CompilerParams(
            collective_id=0, has_side_effects=True, vmem_limit_bytes=48 * 1024 * 1024
        ),
    )(*(a if i == 5 else pltpu.with_memory_space_constraint(a, pltpu.HBM) for i, a in enumerate(operands)))
    return pl.pallas_call(
        product,
        out_shape=jax.ShapeDtypeStruct((MEMBERS, 8, 256), F32),
        in_specs=[vmem, vmem],
        out_specs=vmem,
        compiler_params=pltpu.CompilerParams(vmem_limit_bytes=16 * 1024 * 1024),
    )(second, middle)


def solution(mesh):
    return jax.shard_map(
        shards,
        mesh=mesh,
        in_specs=(
            P("member", "region", "tile"),
            P("region", "tile"),
            P(None, "region", "tile"),
            P("region", "tile"),
            P("region", "tile"),
            P("region", "tile"),
            P("region", "tile"),
        ),
        out_specs=P(None, "region", ("tile", "member")),
        check_vma=False,
    )
```

```python
import functools
import math

import jax
import jax.numpy as jnp
from jax import lax
from jax.experimental import pallas as pl
from jax.experimental.pallas import tpu as pltpu
from jax.sharding import PartitionSpec as P

EXACT = lax.Precision.HIGHEST
MESH = pl.DeviceIdType.MESH
F32 = jnp.float32
BF16 = jnp.bfloat16
MEMBERS = 80
TILES, SPLIT, REGIONS = 8, 4, 16
PART = MEMBERS // SPLIT
NT = (((1,), (1,)), ((), ()))


def rem(a, n):
    return lax.rem(a, n)


def iota(shape, dim):
    return lax.broadcasted_iota(jnp.int32, shape, dim)


def halves(a):
    high = a.astype(BF16)
    low = (a - high.astype(F32)).astype(BF16)
    return high, low


def left_operand(a):
    lane = iota(a.shape, 1)
    high = a.astype(BF16).astype(F32)
    low = a - high
    turned = pltpu.roll(high, MEMBERS, 1)
    one = jnp.where(lane < MEMBERS, high, turned)
    two = jnp.where(lane < 32, turned, pltpu.roll(low, 32, 1))
    return jnp.concatenate([one, two], axis=1).astype(BF16)


def spot(a, j):
    return jnp.broadcast_to(a[j : j + 1, :], (8, 128))


def eliminated(groups):
    lane, sub = iota((8, 128), 1), iota((8, 128), 0)
    groups, finished = list(groups), []
    for b in range(0, 10, 2):
        base = 8 * b
        block = (lane >= base) & (lane < base + 16)
        columns = [
            [jnp.broadcast_to(groups[g][:, base + j : base + j + 1], (8, 128)) for j in range(16)]
            for g in range(b, 10)
        ]
        square = [list(columns[0]), list(columns[1])]
        here = [
            jnp.where(block, jnp.where(lane - base == sub + 8 * i, 1.0, 0.0), groups[b + i]) for i in range(2)
        ]
        pivots, inverses = [None, None], [None, None]
        for j in range(16):
            own, s = divmod(j, 8)
            inverse = 1.0 / spot(square[own][j], s)
            pivots[own] = square[own][j] if s == 0 else jnp.where(sub == s, square[own][j], pivots[own])
            inverses[own] = inverse if s == 0 else jnp.where(sub == s, inverse, inverses[own])
            if j == 15:
                break
            across = {k: spot(square[own][k], s) for k in range(j + 1, 16)}
            row = spot(here[own], s)
            for i in range(own, 2):
                if i == own and s == 7:
                    continue
                factor = square[i][j] * inverse
                if i == own:
                    factor = jnp.where(sub > s, factor, 0.0)
                for k in range(j + 1, 16):
                    square[i][k] = square[i][k] - factor * across[k]
                here[i] = here[i] - factor * row
        finished += [here[i] * lax.rsqrt(pivots[i]) for i in range(2)]
        if b == 8:
            break
        solved = [here[i] * inverses[i] for i in range(2)]
        for j in range(15, 0, -1):
            own, s = divmod(j, 8)
            row = spot(solved[own], s)
            for i in range(own + 1):
                if i == own and s == 0:
                    continue
                factor = square[i][j] * inverses[i]
                if i == own:
                    factor = jnp.where(sub < s, factor, 0.0)
                solved[i] = solved[i] - factor * row
        rows = [spot(solved[j // 8], j % 8) for j in range(16)]
        for g in range(b + 2, 10):
            terms = [c * row for c, row in zip(columns[g - b], rows)]
            while len(terms) > 1:
                terms = [p + q for p, q in zip(terms[::2], terms[1::2])]
            groups[g] = jnp.where(block, 0.0, groups[g]) - terms[0]
    return finished


def transform_rows(system_ref):
    lane, sub = iota((8, 128), 1), iota((8, 128), 0)
    groups = [
        system_ref[8 * g : 8 * g + 8, :] + jnp.where(lane == sub + 8 * g, MEMBERS - 1.0, 0.0) for g in range(10)
    ]
    weights, mean = jnp.zeros((8, 128), F32), jnp.zeros((8, 128), F32)
    centered = []
    for g, rows in enumerate(eliminated(groups)):
        partial = jnp.broadcast_to(rows[:, MEMBERS : MEMBERS + 1], (8, 128))
        inverse = jnp.where(lane <= sub + 8 * g, rows, 0.0)
        average = jnp.broadcast_to(jnp.sum(inverse, axis=1, keepdims=True), (8, 128)) * (1.0 / MEMBERS)
        weights = weights + partial * inverse
        mean = mean + partial * average
        centered.append(math.sqrt(MEMBERS - 1.0) * (inverse - average))
    shift = jnp.sum(weights - mean, axis=0, keepdims=True) + 1.0 / MEMBERS
    return jnp.concatenate([jnp.where(lane < MEMBERS, c + shift, 0.0) for c in centered], axis=0)


def kernel(
    bg, cell_in, wgt_in, val_in, err_in, cnt, bat_in, second, xout,
    cell, wgt, val, err, bat, bgv, x, xcat, halo, from_left, from_right, mine, priors, full, spread, parts, shares,
    own, zone, bslots, bfull, mixed, cslots, system, own2, zone2, mixed2, cslots2, system2,
    load_sem, bulk_s, bulk_r, halo_s, left_r, right_r, prior_s, prior_r, share_s, share_r,
    zone_s, zone_r, b_s, b_r, c_s, c_r, zone2_s, zone2_r, c2_s, c2_r, ring,
):
    t, y, z = lax.axis_index("tile"), lax.axis_index("member"), lax.axis_index("region")
    core, q = rem(t, 2), 4 * y + lax.div(t, 2)

    def at(dt, dy, dz):
        return {
            "tile": rem(t + dt, TILES),
            "member": rem(y + dy, SPLIT),
            "region": rem(z + dz, REGIONS),
        }

    def push(src, dst, s, r, where):
        copy = pltpu.make_async_remote_copy(
            src_ref=src, dst_ref=dst, send_sem=s, recv_sem=r, device_id=where, device_id_type=MESH
        )
        return copy

    plane = [(dt, dy) for dy in range(SPLIT) for dt in range(TILES) if (dt, dy) != (0, 0)]
    near_by = {(dt, 0, 0) for dt in range(1, TILES)} | {(0, dy, 0) for dy in range(1, SPLIT)}
    near_by |= {(dt, dy, 0) for dt in (1, TILES - 1) for dy in range(SPLIT)} | {(0, 0, dz) for dz in (1, 2, 3, 13, 14, 15)}
    plane.sort(key=lambda p: -(min((p[0] + 1) // 2, (TILES - p[0] + 1) // 2) + min(p[1], SPLIT - p[1])))
    peers = sorted(near_by)

    load = pltpu.make_async_copy(bg, bgv, load_sem.at[0])
    load.start()
    small = ((cell_in, cell), (wgt_in, wgt), (val_in, val), (err_in, err), (bat_in, bat))
    small = [pltpu.make_async_copy(src, dst, load_sem.at[2 + i]) for i, (src, dst) in enumerate(small)]
    for copy in small:
        copy.start()
    barrier = pltpu.get_barrier_semaphore()
    for dt, dy, dz in peers:
        pl.semaphore_signal(barrier, inc=1, device_id=at(dt, dy, dz), device_id_type=MESH)

    for copy in small:
        copy.wait()
    place = cell[...]
    at_row, at_col = lax.shift_right_logical(place, 10), place & 1023
    w = [wgt[k] for k in range(4)]
    step = iota((1024, 128), 0) - (at_col - 1)
    taps = jnp.where(step == 0, w[0], jnp.where(step == 1, w[1], jnp.where(step == 2, w[2], jnp.where(step == 3, w[3], 0.0))))
    filled = iota((1, 128), 1) < cnt[0, 0]
    inverse_error = 1.0 / err[...]
    scales = [jnp.where(filled & (bat[...] == b), inverse_error, 0.0) for b in range(2)]
    load.wait()

    packed = jnp.zeros((8, 128), F32)
    lane8 = iota((8, 128), 1)
    for a in range(3):
        count = min(8, PART - 8 * a)
        for r in range(8):
            ends = [bgv[8 * a : 8 * a + count, r, c : c + 128] for c in (896, 0)]
            if count < 8:
                ends = [jnp.concatenate([e, jnp.zeros((8 - count, 128), F32)], axis=0) for e in ends]
            for j, (end, lane) in enumerate(((ends[0], 127), (ends[1], 0), (ends[1], 1))):
                target = 32 * a + 8 * j + r
                packed = jnp.where(lane8 == target, pltpu.roll(end, (target - lane) % 128, 1), packed)
    halo[...] = packed

    rows = bgv[...].reshape(PART * 8, 1024)
    taken = jnp.dot(rows, taps, precision=EXACT, preferred_element_type=F32).reshape(PART, 8, 128)
    chosen = iota((8, 128), 0) == at_row
    mine[...] = jnp.zeros_like(mine)
    mine[0:PART, :] = jnp.sum(jnp.where(chosen[None], taken, 0.0), axis=1)

    near = []
    for d in range(REGIONS):
        other = rem(z - d + REGIONS, REGIONS)
        distance = jnp.full((5, 128), z - other, jnp.int32).astype(F32) * (4.0 / REGIONS)
        near.append(jnp.exp(-0.5 * distance * distance))

    pl.semaphore_wait(barrier, len(peers))

    def tell(step):
        @pl.when(core == 0)
        def _():
            for dz in (3 - step, REGIONS - 3 + step):
                pl.semaphore_signal(ring.at[step], inc=1, device_id=at(0, 0, dz), device_id_type=MESH)

    def heard(step):
        @pl.when(core == 0)
        def _():
            pl.semaphore_wait(ring.at[step], 2)

    tell(0)
    def arrived(like, semaphore):
        pltpu.make_async_copy(like, like, semaphore).wait()

    def go(copy):
        copy.start()

    for i in (2, 1, 3, 0):
        go(push(halo, from_left.at[y], halo_s, left_r, at(1, i, 0)))
        go(push(halo, from_right.at[y], halo_s, right_r, at(TILES - 1, i, 0)))
    for i in range(1, SPLIT):
        go(push(mine, priors.at[y], prior_s, prior_r, at(0, i, 0)))
    priors[y] = mine[...]

    v = [
        jnp.where((t > 0) & (at_col == 0), w[0], 0.0),
        jnp.where(t < TILES - 1, jnp.where(at_col == 1023, w[2], jnp.where(at_col == 1022, w[3], 0.0)), 0.0),
        jnp.where((t < TILES - 1) & (at_col == 1023), w[3], 0.0),
    ]
    block = jnp.concatenate([jnp.where(chosen, value, 0.0) for value in v] + [jnp.zeros((8, 128), F32)], axis=0)
    nothing = jnp.zeros((32, 128), F32)
    spots = jnp.concatenate(
        [jnp.concatenate([block if b == a else nothing for b in range(4)], axis=0) for a in range(3)], axis=1
    )
    heard(0)
    tell(1)
    arrived(from_left, left_r)
    arrived(from_right, right_r)
    from_j0 = (lane8 & 31) < 8
    sides = jnp.concatenate([jnp.where(from_j0, from_left[i], from_right[i]) for i in range(SPLIT)], axis=0)
    extra = jnp.dot(sides, spots, precision=EXACT, preferred_element_type=F32)
    arrived(priors.at[0 : SPLIT - 1], prior_r)
    for i in range(SPLIT):
        for a in range(3):
            full[PART * i + 8 * a : PART * i + 8 * a + 8, :] = (
                priors[i, 8 * a : 8 * a + 8, :] + extra[8 * i : 8 * i + 8, 128 * a : 128 * a + 128]
            )
    ensemble = full[0:MEMBERS, :]
    average = jnp.sum(ensemble, axis=0, keepdims=True) / MEMBERS
    spread[MEMBERS : 128, :] = jnp.where(iota((48, 128), 0) == 0, val[...] - average, 0.0)
    spread[0:MEMBERS, :] = ensemble - average
    picks = []
    for c in range(8):
        start = y * PART + 5 * (c // 2)
        picks.append(spread[pl.ds(start, 8), :] * scales[c % 2])
    products = lax.dot_general(
        jnp.concatenate(picks, axis=0), spread[...], NT, precision=EXACT, preferred_element_type=F32
    )
    for c in range(8):
        parts[c] = products[8 * c : 8 * c + 5, :]
    for d in range(1, TILES):
        to = rem(t + d, TILES)
        go(push(parts.at[to], shares.at[d - 1], share_s, share_r, at(d, 0, 0)))
    for i in range(1, SPLIT):
        to = rem(y + i, SPLIT)
        columns = pl.ds(pl.multiple_of(to * 256, 256), 256)
        go(push(bgv.at[:, :, columns], x.at[pl.ds(y * PART, PART)], bulk_s, bulk_r, at(0, i, 0)))
    keep = pltpu.make_async_copy(
        bgv.at[:, :, pl.ds(pl.multiple_of(y * 256, 256), 256)], x.at[pl.ds(y * PART, PART)], load_sem.at[1]
    )
    keep.start()
    total = parts[t]
    arrived(shares, share_r)
    for d in range(1, TILES):
        total = total + shares[d - 1]
    own[...] = total

    def to_plane(src, slots, s, r):
        return [push(src, slots.at[q], s, r, at(dt, dy, 0)) for dt, dy in plane]

    def to_zone(src, slots, s, r):
        return [push(src, slots.at[d - 1], s, r, at(0, 0, d)) for d in sorted(range(1, REGIONS), key=lambda d: -min(d, REGIONS - d))]

    def mix(src, slots, s, r):
        arrived(slots, r)
        result = near[0] * src[...]
        for d in range(1, REGIONS):
            result = result + near[d] * slots[d - 1]
        return result

    def gathered(src, slots, s, r, owner, whole):
        pl.when(core == owner)(lambda: arrived(slots.at[0:15], r))
        pl.when(core != owner)(lambda: arrived(slots, r))
        for p in range(16):
            whole[5 * p : 5 * p + 5, :] = slots[p]

    b_copies = to_plane(own, bslots, b_s, b_r)
    z_copies = to_zone(own, zone, zone_s, zone_r)
    c_copies = to_plane(mixed, cslots, c_s, c_r)
    z2_copies = to_zone(own2, zone2, zone2_s, zone2_r)
    c2_copies = to_plane(mixed2, cslots2, c2_s, c2_r)

    @pl.when(core == 0)
    def _():
        pl.semaphore_wait(ring.at[1], 2)
        for copy in z_copies:
            copy.start()
        mixed[...] = mix(own, zone, zone_s, zone_r)
        for copy in c_copies:
            copy.start()
        cslots[q] = mixed[...]

    @pl.when(core == 1)
    def _():
        for copy in b_copies:
            copy.start()
        bslots[q] = own[...]

    gathered(own, bslots, b_s, b_r, 1, bfull)
    bfull[MEMBERS : 128, :] = jnp.zeros((48, 128), F32)
    gathered(mixed, cslots, c_s, c_r, 0, system)
    first = transform_rows(system)

    lane, row = iota((MEMBERS, 128), 1), iota((MEMBERS, 128), 0)
    mean_row = jnp.sum(first, axis=0, keepdims=True) / MEMBERS
    system[0:MEMBERS, :] = first - mean_row
    left = jnp.dot(system[pl.ds(5 * q, 8), :], bfull[...], precision=EXACT, preferred_element_type=F32)
    right = jnp.concatenate(
        [system[0:MEMBERS, :], jnp.where(iota((48, 128), 0) == 0, mean_row, 0.0)], axis=0
    )
    stats = lax.dot_general(
        jnp.where(lane8 < MEMBERS, left, 0.0), right, NT, precision=EXACT, preferred_element_type=F32
    )
    own2[...] = jnp.where(lane8 == MEMBERS, left - stats, stats)[0:5, :]

    @pl.when(core == 0)
    def _():
        for copy in z2_copies:
            copy.start()

    @pl.when(core == 0)
    def _():
        mixed2[...] = mix(own2, zone2, zone2_s, zone2_r)
        for copy in c2_copies:
            copy.start()
        cslots2[q] = mixed2[...]

    keep.wait()
    arrived(x.at[0 : (SPLIT - 1) * PART], bulk_r)
    first_left = left_operand(first)
    blank = jnp.zeros((16, 256), BF16)
    for r in range(8):
        high, low = halves(x[:, r, :])
        middle = jnp.dot(first_left, jnp.concatenate([high, low, high, blank], axis=0), preferred_element_type=F32)
        high, low = halves(middle)
        xcat[r, 0:80, :] = high
        xcat[r, 80:160, :] = low
        xcat[r, 160:240, :] = high
        xcat[r, 240:256, :] = blank
    save = pltpu.make_async_copy(xcat, xout, load_sem.at[7])
    save.start()

    gathered(mixed2, cslots2, c2_s, c2_r, 0, system2)
    second[...] = left_operand(transform_rows(system2))
    save.wait()
    arrived(from_left, halo_s)
    arrived(from_right, halo_s)
    arrived(priors.at[0 : SPLIT - 1], prior_s)
    arrived(x.at[0 : (SPLIT - 1) * PART], bulk_s)
    arrived(shares, share_s)

    @pl.when(core == 0)
    def _():
        arrived(zone, zone_s)
        arrived(zone2, zone2_s)
        for semaphore in (c_s, c2_s):
            arrived(cslots, semaphore)
            arrived(cslots.at[0:15], semaphore)

    @pl.when(core == 1)
    def _():
        arrived(bslots, b_s)
        arrived(bslots.at[0:15], b_s)


def product(second, middle, out):
    for r in range(8):
        out[:, r, :] = jnp.dot(second[...], middle[r], preferred_element_type=F32)


def shards(*operands):
    vmem = pl.BlockSpec(memory_space=pltpu.VMEM)
    hbm = pl.BlockSpec(memory_space=pltpu.HBM)
    tile = (8, 128)
    short = (5, 128)
    dma = pltpu.SemaphoreType.DMA
    second, middle = pl.pallas_call(
        kernel,
        out_shape=(jax.ShapeDtypeStruct((MEMBERS, 256), BF16), jax.ShapeDtypeStruct((8, 256, 256), BF16)),
        in_specs=[hbm] * 5 + [pl.BlockSpec(memory_space=pltpu.SMEM), hbm],
        out_specs=(vmem, pl.BlockSpec(memory_space=pl.ANY)),
        scratch_shapes=[
            pltpu.VMEM((1, 128), jnp.int32),
            pltpu.VMEM((4, 1, 128), F32),
            pltpu.VMEM((1, 128), F32),
            pltpu.VMEM((1, 128), F32),
            pltpu.VMEM((1, 128), jnp.int32),
            pltpu.VMEM((PART, 8, 1024), F32),
            pltpu.VMEM((MEMBERS, 8, 256), F32),
            pltpu.VMEM((8, 256, 256), BF16),
            pltpu.VMEM(tile, F32),
            pltpu.VMEM((SPLIT, *tile), F32),
            pltpu.VMEM((SPLIT, *tile), F32),
            pltpu.VMEM((24, 128), F32),
            pltpu.VMEM((SPLIT, 24, 128), F32),
            pltpu.VMEM((88, 128), F32),
            pltpu.VMEM((128, 128), F32),
            pltpu.VMEM((TILES, *short), F32),
            pltpu.VMEM((TILES - 1, *short), F32),
            pltpu.VMEM(short, F32),
            pltpu.VMEM((REGIONS - 1, *short), F32),
            pltpu.VMEM((16, *short), F32),
            pltpu.VMEM((128, 128), F32),
            pltpu.VMEM(short, F32),
            pltpu.VMEM((16, *short), F32),
            pltpu.VMEM((88, 128), F32),
            pltpu.VMEM(short, F32),
            pltpu.VMEM((REGIONS - 1, *short), F32),
            pltpu.VMEM(short, F32),
            pltpu.VMEM((16, *short), F32),
            pltpu.VMEM((88, 128), F32),
            dma((8,)),
            *[dma] * 19,
            pltpu.SemaphoreType.REGULAR((2,)),
        ],
        compiler_params=pltpu.CompilerParams(
            collective_id=0, has_side_effects=True, vmem_limit_bytes=48 * 1024 * 1024
        ),
    )(*(a if i == 5 else pltpu.with_memory_space_constraint(a, pltpu.HBM) for i, a in enumerate(operands)))
    return pl.pallas_call(
        product,
        out_shape=jax.ShapeDtypeStruct((MEMBERS, 8, 256), F32),
        in_specs=[vmem, vmem],
        out_specs=vmem,
        compiler_params=pltpu.CompilerParams(vmem_limit_bytes=16 * 1024 * 1024),
    )(second, middle)


def solution(mesh):
    return jax.shard_map(
        shards,
        mesh=mesh,
        in_specs=(
            P("member", "region", "tile"),
            P("region", "tile"),
            P(None, "region", "tile"),
            P("region", "tile"),
            P("region", "tile"),
            P("region", "tile"),
            P("region", "tile"),
        ),
        out_specs=P(None, "region", ("tile", "member")),
        check_vma=False,
    )
```

```python
import functools
import math

import jax
import jax.numpy as jnp
from jax import lax
from jax.experimental import pallas as pl
from jax.experimental.pallas import tpu as pltpu
from jax.sharding import PartitionSpec as P

EXACT = lax.Precision.HIGHEST
MESH = pl.DeviceIdType.MESH
F32 = jnp.float32
BF16 = jnp.bfloat16
MEMBERS = 80
TILES, SPLIT, REGIONS = 8, 4, 16
PART = MEMBERS // SPLIT
NT = (((1,), (1,)), ((), ()))


def rem(a, n):
    return lax.rem(a, n)


def iota(shape, dim):
    return lax.broadcasted_iota(jnp.int32, shape, dim)


def halves(a):
    high = a.astype(BF16)
    low = (a - high.astype(F32)).astype(BF16)
    return high, low


def left_operand(a):
    lane = iota(a.shape, 1)
    high = a.astype(BF16).astype(F32)
    low = a - high
    turned = pltpu.roll(high, MEMBERS, 1)
    one = jnp.where(lane < MEMBERS, high, turned)
    two = jnp.where(lane < 32, turned, pltpu.roll(low, 32, 1))
    return jnp.concatenate([one, two], axis=1).astype(BF16)


def spot(a, j):
    return jnp.broadcast_to(a[j : j + 1, :], (8, 128))


def eliminated(groups):
    lane, sub = iota((8, 128), 1), iota((8, 128), 0)
    groups, finished = list(groups), []
    for b in range(0, 10, 2):
        base = 8 * b
        block = (lane >= base) & (lane < base + 16)
        columns = [
            [jnp.broadcast_to(groups[g][:, base + j : base + j + 1], (8, 128)) for j in range(16)]
            for g in range(b, 10)
        ]
        square = [list(columns[0]), list(columns[1])]
        here = [
            jnp.where(block, jnp.where(lane - base == sub + 8 * i, 1.0, 0.0), groups[b + i]) for i in range(2)
        ]
        pivots, inverses = [None, None], [None, None]
        for j in range(16):
            own, s = divmod(j, 8)
            inverse = 1.0 / spot(square[own][j], s)
            pivots[own] = square[own][j] if s == 0 else jnp.where(sub == s, square[own][j], pivots[own])
            inverses[own] = inverse if s == 0 else jnp.where(sub == s, inverse, inverses[own])
            if j == 15:
                break
            across = {k: spot(square[own][k], s) for k in range(j + 1, 16)}
            row = spot(here[own], s)
            for i in range(own, 2):
                if i == own and s == 7:
                    continue
                below = jnp.where(sub > s, square[i][j], 0.0) if i == own else square[i][j]
                factor = below * inverse
                square[i][j + 1] = square[i][j + 1] - (below * across[j + 1]) * inverse
                for k in range(j + 2, 16):
                    square[i][k] = square[i][k] - factor * across[k]
                here[i] = here[i] - factor * row
        finished += [here[i] * lax.rsqrt(pivots[i]) for i in range(2)]
        if b == 8:
            break
        solved = [here[i] * inverses[i] for i in range(2)]
        for j in range(15, 0, -1):
            own, s = divmod(j, 8)
            row = spot(solved[own], s)
            for i in range(own + 1):
                if i == own and s == 0:
                    continue
                factor = square[i][j] * inverses[i]
                if i == own:
                    factor = jnp.where(sub < s, factor, 0.0)
                solved[i] = solved[i] - factor * row
        rows = [spot(solved[j // 8], j % 8) for j in range(16)]
        for g in range(b + 2, 10):
            terms = [c * row for c, row in zip(columns[g - b], rows)]
            while len(terms) > 1:
                terms = [p + q for p, q in zip(terms[::2], terms[1::2])]
            groups[g] = jnp.where(block, 0.0, groups[g]) - terms[0]
    return finished


def transform_rows(system_ref):
    lane, sub = iota((8, 128), 1), iota((8, 128), 0)
    groups = [
        system_ref[8 * g : 8 * g + 8, :] + jnp.where(lane == sub + 8 * g, MEMBERS - 1.0, 0.0) for g in range(10)
    ]
    weights, mean = jnp.zeros((8, 128), F32), jnp.zeros((8, 128), F32)
    centered = []
    for g, rows in enumerate(eliminated(groups)):
        partial = jnp.broadcast_to(rows[:, MEMBERS : MEMBERS + 1], (8, 128))
        inverse = jnp.where(lane <= sub + 8 * g, rows, 0.0)
        average = jnp.broadcast_to(jnp.sum(inverse, axis=1, keepdims=True), (8, 128)) * (1.0 / MEMBERS)
        weights = weights + partial * inverse
        mean = mean + partial * average
        centered.append(math.sqrt(MEMBERS - 1.0) * (inverse - average))
    shift = jnp.sum(weights - mean, axis=0, keepdims=True) + 1.0 / MEMBERS
    return jnp.concatenate([jnp.where(lane < MEMBERS, c + shift, 0.0) for c in centered], axis=0)


def kernel(
    bg, cell_in, wgt_in, val_in, err_in, cnt, bat_in, second, xout,
    cell, wgt, val, err, bat, bgv, x, xcat, halo, from_left, from_right, mine, priors, full, spread, parts, shares,
    own, zone, bslots, bfull, mixed, cslots, system, own2, zone2, mixed2, cslots2, system2,
    load_sem, bulk_s, bulk_r, halo_s, left_r, right_r, prior_s, prior_r, share_s, share_r,
    zone_s, zone_r, b_s, b_r, c_s, c_r, zone2_s, zone2_r, c2_s, c2_r, ring,
):
    t, y, z = lax.axis_index("tile"), lax.axis_index("member"), lax.axis_index("region")
    core, q = rem(t, 2), 4 * y + lax.div(t, 2)

    def at(dt, dy, dz):
        return {
            "tile": rem(t + dt, TILES),
            "member": rem(y + dy, SPLIT),
            "region": rem(z + dz, REGIONS),
        }

    def push(src, dst, s, r, where):
        copy = pltpu.make_async_remote_copy(
            src_ref=src, dst_ref=dst, send_sem=s, recv_sem=r, device_id=where, device_id_type=MESH
        )
        return copy

    def hops(dt, dy, dz):
        return min((dt + 1) // 2, (TILES - dt + 1) // 2) + min(dy, SPLIT - dy) + min(dz, REGIONS - dz)

    plane = [(dt, dy) for dy in range(SPLIT) for dt in range(TILES) if (dt, dy) != (0, 0)]
    near_by = {(dt, 0, 0) for dt in range(1, TILES)} | {(0, dy, 0) for dy in range(1, SPLIT)}
    near_by |= {(dt, dy, 0) for dt in (1, TILES - 1) for dy in range(SPLIT)} | {(0, 0, dz) for dz in (1, 2, 3, 13, 14, 15)}
    plane.sort(key=lambda p: -(min((p[0] + 1) // 2, (TILES - p[0] + 1) // 2) + min(p[1], SPLIT - p[1])))
    peers = sorted(near_by, key=lambda p: -hops(*p))

    barrier = pltpu.get_barrier_semaphore()
    for dt, dy, dz in peers:
        pl.semaphore_signal(barrier, inc=1, device_id=at(dt, dy, dz), device_id_type=MESH)
    load = pltpu.make_async_copy(bg, bgv, load_sem.at[0])
    load.start()
    small = ((cell_in, cell), (wgt_in, wgt), (val_in, val), (err_in, err), (bat_in, bat))
    small = [pltpu.make_async_copy(src, dst, load_sem.at[2 + i]) for i, (src, dst) in enumerate(small)]
    for copy in small:
        copy.start()

    for copy in small:
        copy.wait()
    place = cell[...]
    at_row, at_col = lax.shift_right_logical(place, 10), place & 1023
    w = [wgt[k] for k in range(4)]
    step = iota((1024, 128), 0) - (at_col - 1)
    taps = jnp.where(step == 0, w[0], jnp.where(step == 1, w[1], jnp.where(step == 2, w[2], jnp.where(step == 3, w[3], 0.0))))
    filled = iota((1, 128), 1) < cnt[0, 0]
    inverse_error = 1.0 / err[...]
    scales = [jnp.where(filled & (bat[...] == b), inverse_error, 0.0) for b in range(2)]
    load.wait()

    packed = jnp.zeros((8, 128), F32)
    lane8 = iota((8, 128), 1)
    for a in range(3):
        count = min(8, PART - 8 * a)
        for r in range(8):
            ends = [bgv[8 * a : 8 * a + count, r, c : c + 128] for c in (896, 0)]
            if count < 8:
                ends = [jnp.concatenate([e, jnp.zeros((8 - count, 128), F32)], axis=0) for e in ends]
            for j, (end, lane) in enumerate(((ends[0], 127), (ends[1], 0), (ends[1], 1))):
                target = 32 * a + 8 * j + r
                packed = jnp.where(lane8 == target, pltpu.roll(end, (target - lane) % 128, 1), packed)
    halo[...] = packed

    rows = bgv[...].reshape(PART * 8, 1024)
    taken = jnp.dot(rows, taps, precision=EXACT, preferred_element_type=F32).reshape(PART, 8, 128)
    chosen = iota((8, 128), 0) == at_row
    mine[...] = jnp.zeros_like(mine)
    mine[0:PART, :] = jnp.sum(jnp.where(chosen[None], taken, 0.0), axis=1)

    near = []
    for d in range(REGIONS):
        other = rem(z - d + REGIONS, REGIONS)
        distance = jnp.full((5, 128), z - other, jnp.int32).astype(F32) * (4.0 / REGIONS)
        near.append(jnp.exp(-0.5 * distance * distance))

    pl.semaphore_wait(barrier, len(peers))

    def tell(step):
        @pl.when(core == 0)
        def _():
            for dz in (3 - step, REGIONS - 3 + step):
                pl.semaphore_signal(ring.at[step], inc=1, device_id=at(0, 0, dz), device_id_type=MESH)

    def heard(step):
        @pl.when(core == 0)
        def _():
            pl.semaphore_wait(ring.at[step], 2)

    tell(0)
    def arrived(like, semaphore):
        pltpu.make_async_copy(like, like, semaphore).wait()

    def go(copy):
        copy.start()

    for i in (2, 1, 3, 0):
        go(push(halo, from_left.at[y], halo_s, left_r, at(1, i, 0)))
        go(push(halo, from_right.at[y], halo_s, right_r, at(TILES - 1, i, 0)))
    for i in (2, 1, 3):
        go(push(mine, priors.at[y], prior_s, prior_r, at(0, i, 0)))
    priors[y] = mine[...]

    v = [
        jnp.where((t > 0) & (at_col == 0), w[0], 0.0),
        jnp.where(t < TILES - 1, jnp.where(at_col == 1023, w[2], jnp.where(at_col == 1022, w[3], 0.0)), 0.0),
        jnp.where((t < TILES - 1) & (at_col == 1023), w[3], 0.0),
    ]
    block = jnp.concatenate([jnp.where(chosen, value, 0.0) for value in v] + [jnp.zeros((8, 128), F32)], axis=0)
    nothing = jnp.zeros((32, 128), F32)
    spots = jnp.concatenate(
        [jnp.concatenate([block if b == a else nothing for b in range(4)], axis=0) for a in range(3)], axis=1
    )
    heard(0)
    tell(1)
    arrived(from_left, left_r)
    arrived(from_right, right_r)
    from_j0 = (lane8 & 31) < 8
    sides = jnp.concatenate([jnp.where(from_j0, from_left[i], from_right[i]) for i in range(SPLIT)], axis=0)
    extra = jnp.dot(sides, spots, precision=EXACT, preferred_element_type=F32)
    arrived(priors.at[0 : SPLIT - 1], prior_r)
    for i in range(SPLIT):
        for a in range(3):
            full[PART * i + 8 * a : PART * i + 8 * a + 8, :] = (
                priors[i, 8 * a : 8 * a + 8, :] + extra[8 * i : 8 * i + 8, 128 * a : 128 * a + 128]
            )
    ensemble = full[0:MEMBERS, :]
    average = jnp.sum(ensemble, axis=0, keepdims=True) / MEMBERS
    spread[MEMBERS : 128, :] = jnp.where(iota((48, 128), 0) == 0, val[...] - average, 0.0)
    spread[0:MEMBERS, :] = ensemble - average
    picks = []
    for c in range(8):
        start = y * PART + 5 * (c // 2)
        picks.append(spread[pl.ds(start, 8), :] * scales[c % 2])
    products = lax.dot_general(
        jnp.concatenate(picks, axis=0), spread[...], NT, precision=EXACT, preferred_element_type=F32
    )
    for c in range(8):
        parts[c] = products[8 * c : 8 * c + 5, :]
    for d in (4, 3, 5, 2, 6, 1, 7):
        to = rem(t + d, TILES)
        go(push(parts.at[to], shares.at[d - 1], share_s, share_r, at(d, 0, 0)))
    for i in range(1, SPLIT):
        to = rem(y + i, SPLIT)
        columns = pl.ds(pl.multiple_of(to * 256, 256), 256)
        go(push(bgv.at[:, :, columns], x.at[pl.ds(y * PART, PART)], bulk_s, bulk_r, at(0, i, 0)))
    keep = pltpu.make_async_copy(
        bgv.at[:, :, pl.ds(pl.multiple_of(y * 256, 256), 256)], x.at[pl.ds(y * PART, PART)], load_sem.at[1]
    )
    keep.start()
    total = parts[t]
    arrived(shares, share_r)
    for d in range(1, TILES):
        total = total + shares[d - 1]
    own[...] = total

    def to_plane(src, slots, s, r):
        return [push(src, slots.at[q], s, r, at(dt, dy, 0)) for dt, dy in plane]

    def to_zone(src, slots, s, r):
        return [push(src, slots.at[d - 1], s, r, at(0, 0, d)) for d in sorted(range(1, REGIONS), key=lambda d: -min(d, REGIONS - d))]

    def mix(src, slots, s, r):
        arrived(slots, r)
        result = near[0] * src[...]
        for d in range(1, REGIONS):
            result = result + near[d] * slots[d - 1]
        return result

    def gathered(src, slots, s, r, owner, whole):
        pl.when(core == owner)(lambda: arrived(slots.at[0:15], r))
        pl.when(core != owner)(lambda: arrived(slots, r))
        for p in range(16):
            whole[5 * p : 5 * p + 5, :] = slots[p]

    b_copies = to_plane(own, bslots, b_s, b_r)
    z_copies = to_zone(own, zone, zone_s, zone_r)
    c_copies = to_plane(mixed, cslots, c_s, c_r)
    z2_copies = to_zone(own2, zone2, zone2_s, zone2_r)
    c2_copies = to_plane(mixed2, cslots2, c2_s, c2_r)

    @pl.when(core == 0)
    def _():
        pl.semaphore_wait(ring.at[1], 2)
        for copy in z_copies:
            copy.start()
        mixed[...] = mix(own, zone, zone_s, zone_r)
        for copy in c_copies:
            copy.start()
        cslots[q] = mixed[...]

    @pl.when(core == 1)
    def _():
        for copy in b_copies:
            copy.start()
        bslots[q] = own[...]

    gathered(own, bslots, b_s, b_r, 1, bfull)
    bfull[MEMBERS : 128, :] = jnp.zeros((48, 128), F32)
    gathered(mixed, cslots, c_s, c_r, 0, system)
    first = transform_rows(system)

    lane, row = iota((MEMBERS, 128), 1), iota((MEMBERS, 128), 0)
    mean_row = jnp.sum(first, axis=0, keepdims=True) / MEMBERS
    system[0:MEMBERS, :] = first - mean_row
    left = jnp.dot(system[pl.ds(5 * q, 8), :], bfull[...], precision=EXACT, preferred_element_type=F32)
    right = jnp.concatenate(
        [system[0:MEMBERS, :], jnp.where(iota((48, 128), 0) == 0, mean_row, 0.0)], axis=0
    )
    stats = lax.dot_general(
        jnp.where(lane8 < MEMBERS, left, 0.0), right, NT, precision=EXACT, preferred_element_type=F32
    )
    own2[...] = jnp.where(lane8 == MEMBERS, left - stats, stats)[0:5, :]

    @pl.when(core == 0)
    def _():
        for copy in z2_copies:
            copy.start()

    @pl.when(core == 0)
    def _():
        mixed2[...] = mix(own2, zone2, zone2_s, zone2_r)
        for copy in c2_copies:
            copy.start()
        cslots2[q] = mixed2[...]

    keep.wait()
    arrived(x.at[0 : (SPLIT - 1) * PART], bulk_r)
    first_left = left_operand(first)
    blank = jnp.zeros((16, 256), BF16)
    for r in range(8):
        high, low = halves(x[:, r, :])
        middle = jnp.dot(first_left, jnp.concatenate([high, low, high, blank], axis=0), preferred_element_type=F32)
        high, low = halves(middle)
        xcat[r, 0:80, :] = high
        xcat[r, 80:160, :] = low
        xcat[r, 160:240, :] = high
        xcat[r, 240:256, :] = blank
    save = pltpu.make_async_copy(xcat, xout, load_sem.at[7])
    save.start()

    gathered(mixed2, cslots2, c2_s, c2_r, 0, system2)
    second[...] = left_operand(transform_rows(system2))
    save.wait()
    arrived(from_left, halo_s)
    arrived(from_right, halo_s)
    arrived(priors.at[0 : SPLIT - 1], prior_s)
    arrived(x.at[0 : (SPLIT - 1) * PART], bulk_s)
    arrived(shares, share_s)

    @pl.when(core == 0)
    def _():
        arrived(zone, zone_s)
        arrived(zone2, zone2_s)
        for semaphore in (c_s, c2_s):
            arrived(cslots, semaphore)
            arrived(cslots.at[0:15], semaphore)

    @pl.when(core == 1)
    def _():
        arrived(bslots, b_s)
        arrived(bslots.at[0:15], b_s)


def product(second, middle, out):
    for r in range(8):
        out[:, r, :] = jnp.dot(second[...], middle[r], preferred_element_type=F32)


def shards(*operands):
    vmem = pl.BlockSpec(memory_space=pltpu.VMEM)
    hbm = pl.BlockSpec(memory_space=pltpu.HBM)
    tile = (8, 128)
    short = (5, 128)
    dma = pltpu.SemaphoreType.DMA
    second, middle = pl.pallas_call(
        kernel,
        out_shape=(jax.ShapeDtypeStruct((MEMBERS, 256), BF16), jax.ShapeDtypeStruct((8, 256, 256), BF16)),
        in_specs=[hbm] * 5 + [pl.BlockSpec(memory_space=pltpu.SMEM), hbm],
        out_specs=(vmem, pl.BlockSpec(memory_space=pl.ANY)),
        scratch_shapes=[
            pltpu.VMEM((1, 128), jnp.int32),
            pltpu.VMEM((4, 1, 128), F32),
            pltpu.VMEM((1, 128), F32),
            pltpu.VMEM((1, 128), F32),
            pltpu.VMEM((1, 128), jnp.int32),
            pltpu.VMEM((PART, 8, 1024), F32),
            pltpu.VMEM((MEMBERS, 8, 256), F32),
            pltpu.VMEM((8, 256, 256), BF16),
            pltpu.VMEM(tile, F32),
            pltpu.VMEM((SPLIT, *tile), F32),
            pltpu.VMEM((SPLIT, *tile), F32),
            pltpu.VMEM((24, 128), F32),
            pltpu.VMEM((SPLIT, 24, 128), F32),
            pltpu.VMEM((88, 128), F32),
            pltpu.VMEM((128, 128), F32),
            pltpu.VMEM((TILES, *short), F32),
            pltpu.VMEM((TILES - 1, *short), F32),
            pltpu.VMEM(short, F32),
            pltpu.VMEM((REGIONS - 1, *short), F32),
            pltpu.VMEM((16, *short), F32),
            pltpu.VMEM((128, 128), F32),
            pltpu.VMEM(short, F32),
            pltpu.VMEM((16, *short), F32),
            pltpu.VMEM((88, 128), F32),
            pltpu.VMEM(short, F32),
            pltpu.VMEM((REGIONS - 1, *short), F32),
            pltpu.VMEM(short, F32),
            pltpu.VMEM((16, *short), F32),
            pltpu.VMEM((88, 128), F32),
            dma((8,)),
            *[dma] * 19,
            pltpu.SemaphoreType.REGULAR((2,)),
        ],
        compiler_params=pltpu.CompilerParams(
            collective_id=0, has_side_effects=True, vmem_limit_bytes=48 * 1024 * 1024
        ),
    )(*(a if i == 5 else pltpu.with_memory_space_constraint(a, pltpu.HBM) for i, a in enumerate(operands)))
    return pl.pallas_call(
        product,
        out_shape=jax.ShapeDtypeStruct((MEMBERS, 8, 256), F32),
        in_specs=[vmem, vmem],
        out_specs=vmem,
        compiler_params=pltpu.CompilerParams(vmem_limit_bytes=16 * 1024 * 1024),
    )(second, middle)


def solution(mesh):
    return jax.shard_map(
        shards,
        mesh=mesh,
        in_specs=(
            P("member", "region", "tile"),
            P("region", "tile"),
            P(None, "region", "tile"),
            P("region", "tile"),
            P("region", "tile"),
            P("region", "tile"),
            P("region", "tile"),
        ),
        out_specs=P(None, "region", ("tile", "member")),
        check_vma=False,
    )
```

```python
import functools
import math

import jax
import jax.numpy as jnp
from jax import lax
from jax.experimental import pallas as pl
from jax.experimental.pallas import tpu as pltpu
from jax.sharding import PartitionSpec as P

EXACT = lax.Precision.HIGHEST
MESH = pl.DeviceIdType.MESH
F32 = jnp.float32
BF16 = jnp.bfloat16
MEMBERS = 80
TILES, SPLIT, REGIONS = 8, 4, 16
PART = MEMBERS // SPLIT
NT = (((1,), (1,)), ((), ()))


def rem(a, n):
    return lax.rem(a, n)


def iota(shape, dim):
    return lax.broadcasted_iota(jnp.int32, shape, dim)


def halves(a):
    high = a.astype(BF16)
    low = (a - high.astype(F32)).astype(BF16)
    return high, low


def left_operand(a):
    lane = iota(a.shape, 1)
    high = a.astype(BF16).astype(F32)
    low = a - high
    turned = pltpu.roll(high, MEMBERS, 1)
    one = jnp.where(lane < MEMBERS, high, turned)
    two = jnp.where(lane < 32, turned, pltpu.roll(low, 32, 1))
    return jnp.concatenate([one, two], axis=1).astype(BF16)


def spot(a, j):
    return jnp.broadcast_to(a[j : j + 1, :], (8, 128))


def eliminated(groups):
    lane, sub = iota((8, 128), 1), iota((8, 128), 0)
    groups, finished = list(groups), []
    for b in range(0, 10, 2):
        base = 8 * b
        block = (lane >= base) & (lane < base + 16)
        columns = [
            [jnp.broadcast_to(groups[g][:, base + j : base + j + 1], (8, 128)) for j in range(16)]
            for g in range(b, 10)
        ]
        square = [list(columns[0]), list(columns[1])]
        here = [
            jnp.where(block, jnp.where(lane - base == sub + 8 * i, 1.0, 0.0), groups[b + i]) for i in range(2)
        ]
        pivots, inverses = [None, None], [None, None]
        for j in range(16):
            own, s = divmod(j, 8)
            inverse = 1.0 / spot(square[own][j], s)
            pivots[own] = square[own][j] if s == 0 else jnp.where(sub == s, square[own][j], pivots[own])
            inverses[own] = inverse if s == 0 else jnp.where(sub == s, inverse, inverses[own])
            if j == 15:
                break
            across = {k: spot(square[own][k], s) for k in range(j + 1, 16)}
            row = spot(here[own], s)
            for i in range(own, 2):
                if i == own and s == 7:
                    continue
                below = jnp.where(sub > s, square[i][j], 0.0) if i == own else square[i][j]
                factor = below * inverse
                square[i][j + 1] = square[i][j + 1] - (below * across[j + 1]) * inverse
                for k in range(j + 2, 16):
                    square[i][k] = square[i][k] - factor * across[k]
                here[i] = here[i] - factor * row
        finished += [here[i] * lax.rsqrt(pivots[i]) for i in range(2)]
        if b == 8:
            break
        solved = [here[i] * inverses[i] for i in range(2)]
        for j in range(15, 0, -1):
            own, s = divmod(j, 8)
            row = spot(solved[own], s)
            for i in range(own + 1):
                if i == own and s == 0:
                    continue
                factor = square[i][j] * inverses[i]
                if i == own:
                    factor = jnp.where(sub < s, factor, 0.0)
                solved[i] = solved[i] - factor * row
        rows = [spot(solved[j // 8], j % 8) for j in range(16)]
        for g in range(b + 2, 10):
            terms = [c * row for c, row in zip(columns[g - b], rows)]
            while len(terms) > 1:
                terms = [p + q for p, q in zip(terms[::2], terms[1::2])]
            groups[g] = jnp.where(block, 0.0, groups[g]) - terms[0]
    return finished


def transform_rows(system_ref):
    lane, sub = iota((8, 128), 1), iota((8, 128), 0)
    groups = [
        system_ref[8 * g : 8 * g + 8, :] + jnp.where(lane == sub + 8 * g, MEMBERS - 1.0, 0.0) for g in range(10)
    ]
    weights, mean = jnp.zeros((8, 128), F32), jnp.zeros((8, 128), F32)
    centered = []
    for g, rows in enumerate(eliminated(groups)):
        partial = jnp.broadcast_to(rows[:, MEMBERS : MEMBERS + 1], (8, 128))
        inverse = jnp.where(lane <= sub + 8 * g, rows, 0.0)
        average = jnp.broadcast_to(jnp.sum(inverse, axis=1, keepdims=True), (8, 128)) * (1.0 / MEMBERS)
        weights = weights + partial * inverse
        mean = mean + partial * average
        centered.append(math.sqrt(MEMBERS - 1.0) * (inverse - average))
    shift = jnp.sum(weights - mean, axis=0, keepdims=True) + 1.0 / MEMBERS
    return jnp.concatenate([jnp.where(lane < MEMBERS, c + shift, 0.0) for c in centered], axis=0)


def kernel(
    bg, cell_in, wgt_in, val_in, err_in, cnt, bat_in, second, xout,
    cell, wgt, val, err, bat, bgv, x, xcat, halo, from_left, from_right, mine, priors, full, spread, parts, shares,
    own, zone, bslots, bfull, mixed, cslots, system, own2, zone2, mixed2, cslots2, system2,
    load_sem, bulk_s, bulk_r, halo_s, left_r, right_r, prior_s, prior_r, share_s, share_r,
    zone_s, zone_r, b_s, b_r, c_s, c_r, zone2_s, zone2_r, c2_s, c2_r, ring,
):
    t, y, z = lax.axis_index("tile"), lax.axis_index("member"), lax.axis_index("region")
    core, q = rem(t, 2), 4 * y + lax.div(t, 2)

    def at(dt, dy, dz):
        return {
            "tile": rem(t + dt, TILES),
            "member": rem(y + dy, SPLIT),
            "region": rem(z + dz, REGIONS),
        }

    def push(src, dst, s, r, where):
        copy = pltpu.make_async_remote_copy(
            src_ref=src, dst_ref=dst, send_sem=s, recv_sem=r, device_id=where, device_id_type=MESH
        )
        return copy

    def hops(dt, dy, dz):
        return min((dt + 1) // 2, (TILES - dt + 1) // 2) + min(dy, SPLIT - dy) + min(dz, REGIONS - dz)

    plane = [(dt, dy) for dy in range(SPLIT) for dt in range(TILES) if (dt, dy) != (0, 0)]
    near_by = {(dt, 0, 0) for dt in range(1, TILES)} | {(0, dy, 0) for dy in range(1, SPLIT)}
    near_by |= {(dt, dy, 0) for dt in (1, TILES - 1) for dy in range(SPLIT)} | {(0, 0, 1), (0, 0, REGIONS - 1)}
    plane.sort(key=lambda p: -(min((p[0] + 1) // 2, (TILES - p[0] + 1) // 2) + min(p[1], SPLIT - p[1])))
    peers = sorted(near_by, key=lambda p: -hops(*p))

    barrier = pltpu.get_barrier_semaphore()
    for dt, dy, dz in peers:
        pl.semaphore_signal(barrier, inc=1, device_id=at(dt, dy, dz), device_id_type=MESH)
    load = pltpu.make_async_copy(bg, bgv, load_sem.at[0])
    load.start()
    small = ((cell_in, cell), (wgt_in, wgt), (val_in, val), (err_in, err), (bat_in, bat))
    small = [pltpu.make_async_copy(src, dst, load_sem.at[2 + i]) for i, (src, dst) in enumerate(small)]
    for copy in small:
        copy.start()

    for copy in small:
        copy.wait()
    place = cell[...]
    at_row, at_col = lax.shift_right_logical(place, 10), place & 1023
    w = [wgt[k] for k in range(4)]
    step = iota((1024, 128), 0) - (at_col - 1)
    taps = jnp.where(step == 0, w[0], jnp.where(step == 1, w[1], jnp.where(step == 2, w[2], jnp.where(step == 3, w[3], 0.0))))
    filled = iota((1, 128), 1) < cnt[0, 0]
    inverse_error = 1.0 / err[...]
    scales = [jnp.where(filled & (bat[...] == b), inverse_error, 0.0) for b in range(2)]
    load.wait()

    packed = jnp.zeros((8, 128), F32)
    lane8 = iota((8, 128), 1)
    for a in range(3):
        count = min(8, PART - 8 * a)
        for r in range(8):
            ends = [bgv[8 * a : 8 * a + count, r, c : c + 128] for c in (896, 0)]
            if count < 8:
                ends = [jnp.concatenate([e, jnp.zeros((8 - count, 128), F32)], axis=0) for e in ends]
            for j, (end, lane) in enumerate(((ends[0], 127), (ends[1], 0), (ends[1], 1))):
                target = 32 * a + 8 * j + r
                packed = jnp.where(lane8 == target, pltpu.roll(end, (target - lane) % 128, 1), packed)
    halo[...] = packed

    rows = bgv[...].reshape(PART * 8, 1024)
    taken = jnp.dot(rows, taps, precision=EXACT, preferred_element_type=F32).reshape(PART, 8, 128)
    chosen = iota((8, 128), 0) == at_row
    mine[...] = jnp.zeros_like(mine)
    mine[0:PART, :] = jnp.sum(jnp.where(chosen[None], taken, 0.0), axis=1)

    near = []
    for d in range(REGIONS):
        other = rem(z - d + REGIONS, REGIONS)
        distance = jnp.full((5, 128), z - other, jnp.int32).astype(F32) * (4.0 / REGIONS)
        near.append(jnp.exp(-0.5 * distance * distance))

    pl.semaphore_wait(barrier, len(peers))

    def tell(step):
        @pl.when(core == 0)
        def _():
            for dz in (1 << step, REGIONS - (1 << step)):
                pl.semaphore_signal(ring.at[step], inc=1, device_id=at(0, 0, dz), device_id_type=MESH)

    def heard(step):
        @pl.when(core == 0)
        def _():
            pl.semaphore_wait(ring.at[step], 2)

    tell(0)
    def arrived(like, semaphore):
        pltpu.make_async_copy(like, like, semaphore).wait()

    def go(copy):
        copy.start()

    for i in (2, 1, 3, 0):
        go(push(halo, from_left.at[y], halo_s, left_r, at(1, i, 0)))
        go(push(halo, from_right.at[y], halo_s, right_r, at(TILES - 1, i, 0)))
    for i in (2, 1, 3):
        go(push(mine, priors.at[y], prior_s, prior_r, at(0, i, 0)))
    priors[y] = mine[...]

    v = [
        jnp.where((t > 0) & (at_col == 0), w[0], 0.0),
        jnp.where(t < TILES - 1, jnp.where(at_col == 1023, w[2], jnp.where(at_col == 1022, w[3], 0.0)), 0.0),
        jnp.where((t < TILES - 1) & (at_col == 1023), w[3], 0.0),
    ]
    block = jnp.concatenate([jnp.where(chosen, value, 0.0) for value in v] + [jnp.zeros((8, 128), F32)], axis=0)
    nothing = jnp.zeros((32, 128), F32)
    spots = jnp.concatenate(
        [jnp.concatenate([block if b == a else nothing for b in range(4)], axis=0) for a in range(3)], axis=1
    )
    heard(0)
    tell(1)
    arrived(from_left, left_r)
    arrived(from_right, right_r)
    from_j0 = (lane8 & 31) < 8
    sides = jnp.concatenate([jnp.where(from_j0, from_left[i], from_right[i]) for i in range(SPLIT)], axis=0)
    extra = jnp.dot(sides, spots, precision=EXACT, preferred_element_type=F32)
    heard(1)
    tell(2)
    arrived(priors.at[0 : SPLIT - 1], prior_r)
    for i in range(SPLIT):
        for a in range(3):
            full[PART * i + 8 * a : PART * i + 8 * a + 8, :] = (
                priors[i, 8 * a : 8 * a + 8, :] + extra[8 * i : 8 * i + 8, 128 * a : 128 * a + 128]
            )
    ensemble = full[0:MEMBERS, :]
    average = jnp.sum(ensemble, axis=0, keepdims=True) / MEMBERS
    spread[MEMBERS : 128, :] = jnp.where(iota((48, 128), 0) == 0, val[...] - average, 0.0)
    spread[0:MEMBERS, :] = ensemble - average
    picks = []
    for c in range(8):
        start = y * PART + 5 * (c // 2)
        picks.append(spread[pl.ds(start, 8), :] * scales[c % 2])
    products = lax.dot_general(
        jnp.concatenate(picks, axis=0), spread[...], NT, precision=EXACT, preferred_element_type=F32
    )
    for c in range(8):
        parts[c] = products[8 * c : 8 * c + 5, :]
    for d in (4, 3, 5, 2, 6, 1, 7):
        to = rem(t + d, TILES)
        go(push(parts.at[to], shares.at[d - 1], share_s, share_r, at(d, 0, 0)))
    for i in range(1, SPLIT):
        to = rem(y + i, SPLIT)
        columns = pl.ds(pl.multiple_of(to * 256, 256), 256)
        go(push(bgv.at[:, :, columns], x.at[pl.ds(y * PART, PART)], bulk_s, bulk_r, at(0, i, 0)))
    keep = pltpu.make_async_copy(
        bgv.at[:, :, pl.ds(pl.multiple_of(y * 256, 256), 256)], x.at[pl.ds(y * PART, PART)], load_sem.at[1]
    )
    keep.start()
    total = parts[t]
    arrived(shares, share_r)
    for d in range(1, TILES):
        total = total + shares[d - 1]
    own[...] = total

    def to_plane(src, slots, s, r):
        return [push(src, slots.at[q], s, r, at(dt, dy, 0)) for dt, dy in plane]

    def to_zone(src, slots, s, r):
        return [push(src, slots.at[d - 1], s, r, at(0, 0, d)) for d in sorted(range(1, REGIONS), key=lambda d: -min(d, REGIONS - d))]

    def mix(src, slots, s, r):
        arrived(slots, r)
        result = near[0] * src[...]
        for d in range(1, REGIONS):
            result = result + near[d] * slots[d - 1]
        return result

    def gathered(src, slots, s, r, owner, whole):
        pl.when(core == owner)(lambda: arrived(slots.at[0:15], r))
        pl.when(core != owner)(lambda: arrived(slots, r))
        for p in range(16):
            whole[5 * p : 5 * p + 5, :] = slots[p]

    b_copies = to_plane(own, bslots, b_s, b_r)
    z_copies = to_zone(own, zone, zone_s, zone_r)
    c_copies = to_plane(mixed, cslots, c_s, c_r)
    z2_copies = to_zone(own2, zone2, zone2_s, zone2_r)
    c2_copies = to_plane(mixed2, cslots2, c2_s, c2_r)

    @pl.when(core == 0)
    def _():
        pl.semaphore_wait(ring.at[2], 2)
        for copy in z_copies:
            copy.start()
        mixed[...] = mix(own, zone, zone_s, zone_r)
        for copy in c_copies:
            copy.start()
        cslots[q] = mixed[...]

    @pl.when(core == 1)
    def _():
        for copy in b_copies:
            copy.start()
        bslots[q] = own[...]

    gathered(own, bslots, b_s, b_r, 1, bfull)
    bfull[MEMBERS : 128, :] = jnp.zeros((48, 128), F32)
    gathered(mixed, cslots, c_s, c_r, 0, system)
    first = transform_rows(system)

    lane, row = iota((MEMBERS, 128), 1), iota((MEMBERS, 128), 0)
    mean_row = jnp.sum(first, axis=0, keepdims=True) / MEMBERS
    system[0:MEMBERS, :] = first - mean_row
    left = jnp.dot(system[pl.ds(5 * q, 8), :], bfull[...], precision=EXACT, preferred_element_type=F32)
    right = jnp.concatenate(
        [system[0:MEMBERS, :], jnp.where(iota((48, 128), 0) == 0, mean_row, 0.0)], axis=0
    )
    stats = lax.dot_general(
        jnp.where(lane8 < MEMBERS, left, 0.0), right, NT, precision=EXACT, preferred_element_type=F32
    )
    own2[...] = jnp.where(lane8 == MEMBERS, left - stats, stats)[0:5, :]

    @pl.when(core == 0)
    def _():
        for copy in z2_copies:
            copy.start()

    @pl.when(core == 0)
    def _():
        mixed2[...] = mix(own2, zone2, zone2_s, zone2_r)
        for copy in c2_copies:
            copy.start()
        cslots2[q] = mixed2[...]

    keep.wait()
    arrived(x.at[0 : (SPLIT - 1) * PART], bulk_r)
    first_left = left_operand(first)
    blank = jnp.zeros((16, 256), BF16)
    for r in range(8):
        high, low = halves(x[:, r, :])
        middle = jnp.dot(first_left, jnp.concatenate([high, low, high, blank], axis=0), preferred_element_type=F32)
        high, low = halves(middle)
        xcat[r, 0:80, :] = high
        xcat[r, 80:160, :] = low
        xcat[r, 160:240, :] = high
        xcat[r, 240:256, :] = blank
    save = pltpu.make_async_copy(xcat, xout, load_sem.at[7])
    save.start()

    gathered(mixed2, cslots2, c2_s, c2_r, 0, system2)
    second[...] = left_operand(transform_rows(system2))
    save.wait()
    arrived(from_left, halo_s)
    arrived(from_right, halo_s)
    arrived(priors.at[0 : SPLIT - 1], prior_s)
    arrived(x.at[0 : (SPLIT - 1) * PART], bulk_s)
    arrived(shares, share_s)

    @pl.when(core == 0)
    def _():
        arrived(zone, zone_s)
        arrived(zone2, zone2_s)
        for semaphore in (c_s, c2_s):
            arrived(cslots, semaphore)
            arrived(cslots.at[0:15], semaphore)

    @pl.when(core == 1)
    def _():
        arrived(bslots, b_s)
        arrived(bslots.at[0:15], b_s)


def product(second, middle, out):
    for r in range(8):
        out[:, r, :] = jnp.dot(second[...], middle[r], preferred_element_type=F32)


def shards(*operands):
    vmem = pl.BlockSpec(memory_space=pltpu.VMEM)
    hbm = pl.BlockSpec(memory_space=pltpu.HBM)
    tile = (8, 128)
    short = (5, 128)
    dma = pltpu.SemaphoreType.DMA
    second, middle = pl.pallas_call(
        kernel,
        out_shape=(jax.ShapeDtypeStruct((MEMBERS, 256), BF16), jax.ShapeDtypeStruct((8, 256, 256), BF16)),
        in_specs=[hbm] * 5 + [pl.BlockSpec(memory_space=pltpu.SMEM), hbm],
        out_specs=(vmem, pl.BlockSpec(memory_space=pl.ANY)),
        scratch_shapes=[
            pltpu.VMEM((1, 128), jnp.int32),
            pltpu.VMEM((4, 1, 128), F32),
            pltpu.VMEM((1, 128), F32),
            pltpu.VMEM((1, 128), F32),
            pltpu.VMEM((1, 128), jnp.int32),
            pltpu.VMEM((PART, 8, 1024), F32),
            pltpu.VMEM((MEMBERS, 8, 256), F32),
            pltpu.VMEM((8, 256, 256), BF16),
            pltpu.VMEM(tile, F32),
            pltpu.VMEM((SPLIT, *tile), F32),
            pltpu.VMEM((SPLIT, *tile), F32),
            pltpu.VMEM((24, 128), F32),
            pltpu.VMEM((SPLIT, 24, 128), F32),
            pltpu.VMEM((88, 128), F32),
            pltpu.VMEM((128, 128), F32),
            pltpu.VMEM((TILES, *short), F32),
            pltpu.VMEM((TILES - 1, *short), F32),
            pltpu.VMEM(short, F32),
            pltpu.VMEM((REGIONS - 1, *short), F32),
            pltpu.VMEM((16, *short), F32),
            pltpu.VMEM((128, 128), F32),
            pltpu.VMEM(short, F32),
            pltpu.VMEM((16, *short), F32),
            pltpu.VMEM((88, 128), F32),
            pltpu.VMEM(short, F32),
            pltpu.VMEM((REGIONS - 1, *short), F32),
            pltpu.VMEM(short, F32),
            pltpu.VMEM((16, *short), F32),
            pltpu.VMEM((88, 128), F32),
            dma((8,)),
            *[dma] * 19,
            pltpu.SemaphoreType.REGULAR((3,)),
        ],
        compiler_params=pltpu.CompilerParams(
            collective_id=0, has_side_effects=True, vmem_limit_bytes=48 * 1024 * 1024
        ),
    )(*(a if i == 5 else pltpu.with_memory_space_constraint(a, pltpu.HBM) for i, a in enumerate(operands)))
    return pl.pallas_call(
        product,
        out_shape=jax.ShapeDtypeStruct((MEMBERS, 8, 256), F32),
        in_specs=[vmem, vmem],
        out_specs=vmem,
        compiler_params=pltpu.CompilerParams(vmem_limit_bytes=16 * 1024 * 1024),
    )(second, middle)


def solution(mesh):
    return jax.shard_map(
        shards,
        mesh=mesh,
        in_specs=(
            P("member", "region", "tile"),
            P("region", "tile"),
            P(None, "region", "tile"),
            P("region", "tile"),
            P("region", "tile"),
            P("region", "tile"),
            P("region", "tile"),
        ),
        out_specs=P(None, "region", ("tile", "member")),
        check_vma=False,
    )
```
